512 devices in a mesh: wide: 64 (over y, z), narrow: 8 (over x, core).
Axes of the slice: x: 4, y: 8, z: 8, core: 2. Of those that a mesh axis runs over, the one named last changes fastest.
Arguments:
- hidden: bfloat16 [16384, 1536], P('wide', 'narrow'), may hold values from -6 to 6
- start_state: bfloat16 [1024, 24, 64, 128], P('wide', 'narrow'), may hold values from -0.59765625 to 0.59765625
- tail_inner: bfloat16 [1024, 3, 1536], P('wide', None, 'narrow'), may hold values from -6 to 6
- tail_shared: bfloat16 [1024, 3, 256], P('wide'), may hold values from -6 to 6
- input_gain: float32 [1536], replicated, may hold values from 0.5 to 1.5
- w_gate_inner: bfloat16 [1536, 3072], P(None, 'narrow'), may hold values from -0.15625 to 0.15625
- w_shared: bfloat16 [1536, 256], P(None, 'narrow'), may hold values from -0.15625 to 0.15625
- w_step: bfloat16 [1536, 24], P(None, 'narrow'), may hold values from -0.15625 to 0.15625
- step_bias: float32 [24], P('narrow'), may hold values from -4 to -1
- decay_log: float32 [24], P('narrow'), may hold values from 0 to 2.5
- conv_inner: bfloat16 [4, 1536], P(None, 'narrow'), may hold values from -3 to 3
- conv_inner_bias: float32 [1536], P('narrow'), may hold values from -1.5 to 1.5
- conv_shared: bfloat16 [4, 256], replicated, may hold values from -3 to 3
- conv_shared_bias: float32 [256], replicated, may hold values from -1.5 to 1.5
- skip_gain: float32 [24], P('narrow'), may hold values from 0.5 to 1.5
- gated_gain: float32 [1536], P('narrow'), may hold values from 0.5 to 1.5
- w_output: bfloat16 [1536, 1536], P('narrow'), may hold values from -0.15625 to 0.15625
- next_gain: float32 [1536], replicated, may hold values from 0.5 to 1.5
- w_next: bfloat16 [1536, 3224], P(None, 'narrow'), may hold values from -0.15625 to 0.15625
- dealing: int32 [1024], replicated, may hold values from 0 to 1023, as said below
- accepted: int32 [1024], replicated, may hold values from 0 to 16
- owners: int32 [1024], replicated, may hold values from 0 to 63, as said below
Outputs:
- new_hidden: bfloat16 [16384, 1536], P('wide', 'narrow')
- next_input: bfloat16 [16384, 3224], P('wide', 'narrow')
- kept_state: bfloat16 [1024, 24, 64, 128], P('wide', 'narrow')
- kept_tail_inner: bfloat16 [1024, 3, 1536], P('wide', None, 'narrow')
- kept_tail_shared: bfloat16 [1024, 3, 256], P('wide')
The draws below stay inside these ranges and needn't reach their ends.
Inputs may be any that keep to these rules, and one draw needn't show every extreme that they name: `dealing`: a permutation of the 1024 requests; slot j lies on index j // 16 of wide. Each owner keeps exactly 16 requests, and the requests of the slots of one index of wide have different owners.
All inputs are finite; a program needn't handle non-finite values.
Results may differ from the reference program's by a relative error of at most 0.02.
Values may be sent and summed in bfloat16 or wider, within the bound.
A program may use at most 64 MiB of HBM per device.

```python
import jax
import jax.numpy as jnp
from jax import lax

D = 1536
P_SIZE = 64
N = 128
K = 4
NEXT = 3224
H = 24
DRAFT = 16
R_DEV = 16
REQ = 1024
TOKENS = 16384
XW = 1536
BCW = 256
N_NARROW = 8


def deal_tables(key):
    folded = jax.random.fold_in(key, 7)
    first, second, third, fourth = jax.random.split(folded, 4)
    wide_count = REQ // R_DEV
    dealing = jax.random.permutation(first, REQ).astype(jnp.int32)
    column_order = jax.random.permutation(second, wide_count).astype(jnp.int32)
    owner_order = jax.random.permutation(third, wide_count).astype(jnp.int32)
    offsets = jax.random.permutation(fourth, wide_count)[:R_DEV].astype(jnp.int32)
    slots = jnp.arange(REQ, dtype=jnp.int32)
    slot_owner = owner_order[(column_order[slots // R_DEV] + offsets[slots % R_DEV]) % wide_count]
    owners = jnp.zeros((REQ,), jnp.int32).at[dealing].set(slot_owner)
    return (dealing, owners)


def draw_dealing(key, part):
    return deal_tables(key)[0]


def draw_owners(key, part):
    return deal_tables(key)[1]


def with_ends(entries, key, smallest, high):
    longest = entries.shape.index(max(entries.shape))
    spots = []
    for shift in (0, 1):
        where = [jax.random.randint(jax.random.fold_in(key, axis), (), 0, length) for axis, length in enumerate(entries.shape)]
        where[longest] = (where[longest] + shift) % entries.shape[longest]
        spots.append(tuple(where))
    return entries.at[spots[0]].set(smallest).at[spots[1]].set(high)


def steps_of(key, shape, cuts, least, high):
    loudness, own = 1.0, jax.random.fold_in(key, 6)
    for axis_at, shards_of in cuts:
        heights = jnp.exp(jax.random.uniform(jax.random.fold_in(own, axis_at), (shards_of,), jnp.float32, least / len(cuts), high / len(cuts)))
        loudness = loudness * jnp.repeat(heights, shape[axis_at] // shards_of).reshape([-1 if axis == axis_at else 1 for axis in range(len(shape))])
    return loudness


def scatter_about(key, dims, deviation, bound, shards=(), held_as=jnp.bfloat16):
    result = deviation * jax.random.normal(key, dims, jnp.float32)
    if shards:
        result = result * steps_of(key, dims, shards, -0.22, 0.18)
    return jnp.clip(result, -bound, bound).astype(held_as)


def setup_inputs(seed: int = 0) -> dict:
    key_of = jax.random.split(jax.random.key(seed), 23)
    return {
        "hidden": scatter_about(key_of[0], (TOKENS, D), 1.0, 6.0, ((0, 64), (1, 8))),
        "start_state": scatter_about(key_of[1], (REQ, H, P_SIZE, N), 0.1, 0.59765625, ((0, 64), (1, 8))),
        "tail_inner": scatter_about(key_of[2], (REQ, K - 1, XW), 1.0, 6.0, ((0, 64), (2, 8))),
        "tail_shared": scatter_about(key_of[3], (REQ, K - 1, BCW), 1.0, 6.0, ((0, 64),)),
        "input_gain": jnp.clip(1.0 + 0.1 * jax.random.normal(key_of[4], (D,), jnp.float32), 0.5, 1.5),
        "w_gate_inner": scatter_about(key_of[5], (D, 2 * XW), D ** -0.5, 0.15625, ((1, 8),)),
        "w_shared": scatter_about(key_of[6], (D, BCW), D ** -0.5, 0.15625, ((1, 8),)),
        "w_step": scatter_about(key_of[7], (D, H), D ** -0.5, 0.15625, ((1, 8),)),
        "step_bias": jnp.clip(-4.0 + 3.0 * jax.random.uniform(key_of[8], (H,), jnp.float32) ** steps_of(key_of[8], (H,), ((0, 8),), -0.2, 0.2), -4.0, -1.0),
        "decay_log": jnp.clip(2.5 * jax.random.uniform(key_of[9], (H,), jnp.float32) ** steps_of(key_of[9], (H,), ((0, 8),), -0.2, 0.2), 0.0, 2.5),
        "conv_inner": scatter_about(key_of[10], (K, XW), K ** -0.5, 3.0, ((1, 8),)),
        "conv_inner_bias": scatter_about(key_of[11], (XW,), 0.3, 1.5, ((0, 8),), jnp.float32),
        "conv_shared": scatter_about(key_of[12], (K, BCW), K ** -0.5, 3.0),
        "conv_shared_bias": scatter_about(key_of[13], (BCW,), 0.3, 1.5, (), jnp.float32),
        "skip_gain": jnp.clip(0.5 + 1.0 * jax.random.uniform(key_of[14], (H,), jnp.float32) ** steps_of(key_of[14], (H,), ((0, 8),), -0.2, 0.2), 0.5, 1.5),
        "gated_gain": jnp.clip(1.0 + 0.1 * jax.random.normal(key_of[15], (XW,), jnp.float32), 0.5, 1.5),
        "w_output": scatter_about(key_of[16], (XW, D), XW ** -0.5, 0.15625, ((0, 8),)),
        "next_gain": jnp.clip(1.0 + 0.1 * jax.random.normal(key_of[17], (D,), jnp.float32), 0.5, 1.5),
        "w_next": scatter_about(key_of[18], (D, NEXT), D ** -0.5, 0.15625, ((1, 8),)),
        "dealing": draw_dealing(jax.random.fold_in(key_of[22], 71), 0),
        "accepted": with_ends(jax.random.randint(key_of[20], (REQ,), 0, DRAFT + 1), jax.random.fold_in(key_of[20], 1), 0, DRAFT).astype(jnp.int32),
        "owners": draw_owners(jax.random.fold_in(key_of[22], 71), 0),
    }


EPSILON = 1e-05
HIGHEST = lax.Precision.HIGHEST

def root_norm(values, gain):
    values = values.astype(jnp.float32)
    factor = lax.rsqrt(lax.optimization_barrier(jnp.mean(values * values, axis=-1, keepdims=True)) + EPSILON)
    return (values * factor * gain).astype(jnp.bfloat16)

def causal_filter(tail, fresh, weight, offset):
    extended = jnp.concatenate([tail, fresh], axis=1)
    length = fresh.shape[1]
    summed = jnp.zeros(fresh.shape, jnp.float32) + offset
    for place in range(weight.shape[0]):
        summed = summed + extended[:, place:place + length].astype(jnp.float32) * weight[place].astype(jnp.float32)
    return (jax.nn.silu(summed), extended)

def pick_rows(extended, accepted_now, count):
    length = extended.shape[1]
    wanted = accepted_now[:, None] + jnp.arange(count, dtype=jnp.int32)[None, :]
    onehot = (wanted[:, :, None] == jnp.arange(length, dtype=jnp.int32)[None, None, :]).astype(jnp.float32)
    return jnp.einsum('rqe,rec->rqc', onehot, extended.astype(jnp.float32), precision=HIGHEST).astype(jnp.bfloat16)

def state_block(inner, shared, step_raw, step_bias, decay_log, skip_gain, start_state, accepted_now):
    states = shared.shape[-1] // 2
    b_part = shared[..., :states]
    c_part = shared[..., states:]
    length = inner.shape[1]
    steps_now = jax.nn.softplus(step_raw.astype(jnp.float32) + step_bias)
    log_decay = steps_now * -jnp.exp(decay_log)
    cumul = jnp.cumsum(log_decay, axis=1)
    prefix = jnp.concatenate([jnp.zeros_like(cumul[:, :1]), cumul], axis=1)
    places = jnp.arange(length, dtype=jnp.int32)
    lower = (places[:, None] >= places[None, :])[None, :, :, None]
    spread = cumul[:, :, None, :] - cumul[:, None, :, :]
    weights = jnp.where(lower, jnp.exp(jnp.where(lower, spread, 0.0)), 0.0) * steps_now[:, None, :, :]
    intersection = jnp.einsum('rtn,rsn->rts', c_part, b_part, precision=HIGHEST)
    mixing = weights * intersection[:, :, :, None]
    state_now = start_state.astype(jnp.float32)
    carried = jnp.einsum('rtn,rhpn->rthp', c_part, state_now, precision=HIGHEST) * jnp.exp(cumul)[:, :, :, None]
    direct = jnp.einsum('rtsh,rshp->rthp', mixing, inner, precision=HIGHEST)
    outputs = carried + direct + skip_gain[:, None] * inner
    chosen = (jnp.arange(length + 1, dtype=jnp.int32)[None, :] == accepted_now[:, None]).astype(jnp.float32)
    ending = jnp.einsum('rk,rkh->rh', chosen, prefix, precision=HIGHEST)
    before = (places[None, :] < accepted_now[:, None])[:, :, None]
    factor = jnp.where(before, jnp.exp(jnp.where(before, ending[:, None, :] - cumul, 0.0)), 0.0) * steps_now
    kept = jnp.exp(ending)[:, :, None, None] * state_now + jnp.einsum('rsh,rshp,rsn->rhpn', factor, inner, b_part, precision=HIGHEST)
    return (outputs, kept.astype(jnp.bfloat16))

def reference(hidden, start_state, tail_inner, tail_shared, input_gain, w_gate_inner, w_shared, w_step, step_bias, decay_log, conv_inner, conv_inner_bias, conv_shared, conv_shared_bias, skip_gain, gated_gain, w_output, next_gain, w_next, dealing, accepted, owners):
    tokens = hidden.shape[0]
    requests = start_state.shape[0]
    heads = start_state.shape[1]
    head_size = start_state.shape[2]
    inner_width = w_output.shape[0]
    length = tokens // requests
    block = inner_width // N_NARROW
    normed_in = root_norm(hidden, input_gain)
    gate_inner = jnp.dot(normed_in, w_gate_inner, preferred_element_type=jnp.float32).astype(jnp.bfloat16)
    shared_in = jnp.dot(normed_in, w_shared, preferred_element_type=jnp.float32).astype(jnp.bfloat16)
    step_raw = jnp.dot(normed_in, w_step, preferred_element_type=jnp.float32).astype(jnp.bfloat16)
    halves = gate_inner.reshape(tokens, N_NARROW, 2, block)
    gate_part = halves[:, :, 0].reshape(tokens, inner_width)
    inner_in = halves[:, :, 1].reshape(tokens, inner_width)
    inner_conv, inner_ext = causal_filter(tail_inner, inner_in.reshape(requests, length, inner_width), conv_inner, conv_inner_bias)
    shared_conv, shared_ext = causal_filter(tail_shared, shared_in.reshape(requests, length, -1), conv_shared, conv_shared_bias)
    accepted_now = accepted[dealing].astype(jnp.int32)
    groups = requests // R_DEV

    def one_group(pieces):
        inner_piece, shared_piece, step_piece, state_piece, accepted_piece = pieces
        return state_block(inner_piece.reshape(R_DEV, length, heads, head_size), shared_piece, step_piece, step_bias, decay_log, skip_gain, state_piece, accepted_piece)
    outputs, kept = lax.map(one_group, (inner_conv.reshape(groups, R_DEV, length, inner_width), shared_conv.reshape(groups, R_DEV, length, -1), step_raw.reshape(groups, R_DEV, length, heads), start_state.reshape((groups, R_DEV) + start_state.shape[1:]), accepted_now.reshape(groups, R_DEV)))
    outputs = outputs.reshape(tokens, inner_width)
    kept = kept.reshape(start_state.shape)
    gated = outputs * jax.nn.silu(gate_part.astype(jnp.float32))
    gated_norm = root_norm(gated, gated_gain)
    summed = jnp.zeros((tokens, hidden.shape[1]), jnp.float32)
    for group_index in range(N_NARROW):
        partial_sum = jnp.dot(gated_norm[:, group_index * block:(group_index + 1) * block], w_output[group_index * block:(group_index + 1) * block], preferred_element_type=jnp.float32).astype(jnp.bfloat16)
        summed = summed + lax.optimization_barrier(partial_sum).astype(jnp.float32)
    new_hidden = (hidden.astype(jnp.float32) + summed).astype(jnp.bfloat16)
    normed_next = root_norm(new_hidden, next_gain)
    next_input = jnp.dot(normed_next, w_next, preferred_element_type=jnp.float32).astype(jnp.bfloat16)
    owner_table = (owners[:, None] == jnp.arange(groups, dtype=jnp.int32)[None, :]).astype(jnp.int32)
    ranking = lax.optimization_barrier(jnp.sum((jnp.cumsum(owner_table, axis=0) - owner_table) * owner_table, axis=1)).astype(jnp.int32)
    target = (owners * R_DEV + ranking).astype(jnp.int32)
    slot_target = target[dealing].astype(jnp.int32)
    kept_state = jnp.zeros_like(start_state).at[slot_target].set(kept)
    kept_tail_inner = jnp.zeros_like(tail_inner).at[slot_target].set(pick_rows(inner_ext, accepted_now, tail_inner.shape[1]))
    kept_tail_shared = jnp.zeros_like(tail_shared).at[slot_target].set(pick_rows(shared_ext, accepted_now, tail_shared.shape[1]))
    return (new_hidden, next_input, kept_state, kept_tail_inner, kept_tail_shared)
```

```python
import functools

import jax
import jax.numpy as jnp
from jax import lax
from jax.experimental import pallas as pl
from jax.experimental.pallas import tpu as pltpu
from jax.sharding import PartitionSpec as P

EPSILON = 1e-05
HIGHEST = lax.Precision.HIGHEST
MESH = pl.DeviceIdType.MESH
F32 = jnp.float32
BF16 = jnp.bfloat16


def fdot(a, b):
    return jnp.dot(a, b, precision=HIGHEST, preferred_element_type=F32)


def bdot(a, b):
    return jnp.dot(a, b, preferred_element_type=F32)


SIDE = 8
FAR = 4
BASE = (0, 0, 16, 32, 44)
STEPS = (4, 12, 16, 16)


def hop_base(dist):
    return jnp.where(dist <= 1, 0, jnp.where(dist == 2, 16, jnp.where(dist == 3, 32, 44)))


def table_values(dealing, owners, accepted, me, per=16):
    T = dealing.shape[1]
    ln = lax.broadcasted_iota(jnp.int32, (1, T), 1)
    sub = lax.broadcasted_iota(jnp.int32, (T, T), 0)
    pick = (sub == dealing).astype(BF16)
    row8 = lax.broadcasted_iota(jnp.int32, (8, T), 0)
    known = jnp.where(row8 == 0, owners, accepted).astype(F32).astype(BF16)
    per_slot = jnp.dot(known, pick, preferred_element_type=F32).astype(jnp.int32)
    owner = per_slot[0:1]
    acc = per_slot[1:2]
    sender = ln >> 4
    ys, zs = sender >> 3, sender & 7
    yo, zo = owner >> 3, owner & 7
    me_y, me_z = me // SIDE, lax.rem(me, SIDE)
    halves = []
    keys, starts = [], []
    for fs, fo, gs, go in ((zs, zo, ys, yo), (ys, yo, zs, zo)):
        d1 = (fo - fs) & 7
        back1 = jnp.where((d1 > FAR) | ((d1 == FAR) & ((go & 1) == 1)), 1, 0)
        dist1 = jnp.where(back1 == 1, SIDE - d1, d1)
        d2 = (go - gs) & 7
        back2 = jnp.where((d2 > FAR) | ((d2 == FAR) & ((fs & 1) == 1)), 1, 0)
        dist2 = jnp.where(back2 == 1, SIDE - d2, d2)
        for group, dist in ((sender * 2 + back1, dist1), (owner * 2 + back2, dist2)):
            start = group * (8 * T)
            starts.append(start.astype(F32))
            keys.append((start + (FAR - dist) * T + ln).astype(F32))
        halves.append((back1, dist1, back2, dist2))
    starts.append((owner * T).astype(F32))
    keys.append((owner * T + dealing).astype(F32))
    stacked = jnp.where(row8 == 0, keys[0], jnp.where(row8 == 1, keys[1], jnp.where(row8 == 2, keys[2], jnp.where(row8 == 3, keys[3], keys[4]))))
    return ln, sender, owner, acc, me_y, me_z, halves, keys, starts, stacked


def finish_tables(ln, sender, owner, acc, me, halves, places):
    T = ln.shape[1]
    lane = lax.broadcasted_iota(jnp.int32, (128, 128), 1)
    sub = lax.broadcasted_iota(jnp.int32, (128, 128), 0)
    t = lax.broadcasted_iota(jnp.int32, (128, 1), 0)
    def to_row(column):
        return jnp.sum(jnp.where(lane == sub, column.astype(F32), 0.0), axis=0, keepdims=True).astype(jnp.int32)
    def lookup(want, key, value, missing):
        return to_row(jnp.max(jnp.where(want == key, value, missing).astype(F32), axis=1, keepdims=True))
    me_y, me_z = me // SIDE, lax.rem(me, SIDE)
    out = []
    for h in (0, 1):
        back1, dist1, back2, dist2 = halves[h]
        pos1, pos2 = places[2 * h], places[2 * h + 1]
        loc = jnp.where(dist1 == 0, ln & 15, 16 + back1 * 48 + hop_base(dist1) + pos1)
        out.append(lookup(me * 32 + t, sender * 32 + back1 * 16 + pos1, ln & 15, 0))
        back_t = jnp.where(t >= 48, 1, 0)
        q = t - 48 * back_t
        hop = jnp.where(q < 4, 4, jnp.where(q < 16, 3, jnp.where(q < 32, 2, 1)))
        i = q - jnp.where(q < 4, 0, jnp.where(q < 16, 4, jnp.where(q < 32, 16, 32)))
        move = jnp.where(back_t == 1, -hop, hop)
        if h == 0:
            dest = ((me_y + move) & 7) * SIDE + me_z
        else:
            dest = me_y * SIDE + ((me_z + move) & 7)
        out.append(lookup(((dest * 2 + back_t) * 8 + hop) * 16 + i, ((owner * 2 + back2) * 8 + dist2) * 16 + pos2, loc, -1))
        out.append(lookup(me * 16 + t, owner * 16 + places[4], jnp.where(dist2 == 0, loc, 128 + back2 * 16 + pos2), 0))
    out.append(lookup(me * 16 + t, ln, acc, 0))
    out.append(out[-1])
    r = lax.broadcasted_iota(jnp.int32, (8, 128), 0)
    table = jnp.zeros((8, 128), jnp.int32)
    for k in range(7):
        table = jnp.where(r == k, out[k], table)
    return table


def table_kernel(dealing_ref, owners_ref, accepted_ref, table_ref, count_ref, columns):
    me = lax.axis_index("wide")
    ln, sender, owner, acc, me_y, me_z, halves, keys, starts, stacked = table_values(
        dealing_ref[...], owners_ref[...], accepted_ref[...], me
    )
    columns[...] = jnp.transpose(stacked)
    total = ln.shape[1]
    chunk = 64

    def count(step, found):
        part = columns[pl.ds(pl.multiple_of(step * chunk, chunk), chunk), :]
        return tuple(
            found[k]
            + jnp.sum(
                jnp.where((part[:, k : k + 1] >= starts[k]) & (part[:, k : k + 1] < keys[k]), 1.0, 0.0),
                axis=0,
                keepdims=True,
            )
            for k in range(5)
        )

    found = lax.fori_loop(
        0, total // chunk, count, tuple(jnp.zeros((1, total), F32) for _ in range(5))
    )
    table_ref[...] = finish_tables(
        ln, sender, owner, acc, me, halves, [places.astype(jnp.int32) for places in found]
    )
    tokens = count_ref.shape[0]
    slot = lax.broadcasted_iota(jnp.int32, (tokens, total), 0) >> 4
    at = lax.broadcasted_iota(jnp.int32, (tokens, total), 1)
    count_ref[...] = jnp.sum(
        jnp.where(at == me * 16 + slot, acc, 0).astype(F32), axis=1, keepdims=True
    ).astype(jnp.int32)


CAPS = (16, 16, 12, 4)
OFFS = (0, 16, 32, 44)
SECOND_OFFS = (0, 4, 16, 32)


class Route:
    def __init__(self, number, table, refs, send_sem, recv_sem, side):
        self.number, self.table, self.send_sem, self.recv_sem, self.side = (
            number, table, send_sem, recv_sem, side
        )
        self.pool, self.lists, self.passing, self.final, self.second = refs

    def neighbour(self, half, back, phase):
        me = lax.axis_index("wide")
        side = self.side
        y, z = me // side, lax.rem(me, side)
        move = side - 1 if back else 1
        if (half == 0) == (phase == 0):
            return y * side + lax.rem(z + move, side)
        return lax.rem(y + move, side) * side + z

    def copy(self, phase, half, back, hop):
        if phase == 0:
            low = 16 + 48 * back
            if hop == 0:
                source = self.lists.at[half, back]
            else:
                source = self.pool.at[half, pl.ds(low + OFFS[hop - 1], CAPS[hop])]
            target = self.pool.at[half, pl.ds(low + OFFS[hop], CAPS[hop])]
        else:
            size = CAPS[3 - hop]
            source = self.second.at[half, back, pl.ds(SECOND_OFFS[hop], size)]
            if hop < 3:
                target = self.passing.at[half, back, pl.ds(SECOND_OFFS[hop], size)]
            else:
                target = self.final.at[half, pl.ds(16 * back, size)]
        at = (((self.number * 2 + phase) * 2 + half) * 2 + back) * 4 + hop
        return pltpu.make_async_remote_copy(
            src_ref=source,
            dst_ref=target,
            send_sem=self.send_sem.at[at],
            recv_sem=self.recv_sem.at[at],
            device_id={"wide": self.neighbour(half, back, phase)},
            device_id_type=MESH,
        )

    def each(self, phase, hop):
        return [self.copy(phase, half, back, hop) for half in (0, 1) for back in (0, 1)]

    def fill(self, blocks, rows):
        for half in (0, 1):
            low = half * rows

            def own(i, carry):
                self.pool[half, i] = blocks[i, low : low + rows, :]
                return carry

            lax.fori_loop(0, 16, own, 0)
            for back in (0, 1):

                def listed(i, carry):
                    self.lists[half, back, i] = blocks[self.table[3 * half, 16 * back + i], low : low + rows, :]
                    return carry

                lax.fori_loop(0, 16, listed, 0)

    def first(self, hop):
        if hop > 0:
            for copy in self.each(0, hop - 1):
                copy.wait_recv()
        if hop < 4:
            for copy in self.each(0, hop):
                copy.start()

    def after(self, hop):
        if hop > 0:
            for copy in self.each(1, hop - 1):
                copy.wait_recv()
        if hop == 4:
            return
        low = SECOND_OFFS[hop]
        size = CAPS[3 - hop]
        known = CAPS[4 - hop] if hop > 0 else 0
        for half in (0, 1):
            for back in (0, 1):

                def merged(i, carry):
                    at = self.table[3 * half + 1, 48 * back + low + i]
                    mine = self.pool[half, jnp.maximum(at, 0)]
                    came = self.passing[half, back, SECOND_OFFS[hop - 1] + i]
                    self.second[half, back, low + i] = jnp.where(at >= 0, mine, came)
                    return carry

                def fresh(i, carry):
                    at = self.table[3 * half + 1, 48 * back + low + i]
                    self.second[half, back, low + i] = self.pool[half, jnp.maximum(at, 0)]
                    return carry

                if known:
                    lax.fori_loop(0, known, merged, 0)
                if known < size:
                    lax.fori_loop(known, size, fresh, 0)
        for copy in self.each(1, hop):
            copy.start()

    def collect(self, blocks, rows):
        for half in (0, 1):
            low = half * rows

            def take(k, carry):
                at = self.table[3 * half + 2, k]
                here = self.pool[half, jnp.where(at < 128, at, 0)]
                came = self.final[half, jnp.where(at < 128, 0, at - 128)]
                blocks[k, low : low + rows, :] = jnp.where(at < 128, here, came)
                return carry

            lax.fori_loop(0, 16, take, 0)

    def drain(self):
        for phase in (0, 1):
            for hop in range(4):
                for copy in self.each(phase, hop):
                    copy.wait_send()


def layer_kernel(
    count,
    side,
    table_ref,
    acc_ref,
    hidden_ref,
    start_ref,
    tail_inner_ref,
    tail_shared_ref,
    gain_ref,
    w_gate_ref,
    w_inner_ref,
    w_small_ref,
    bias_ref,
    decay_ref,
    conv_inner_ref,
    conv_inner_bias_ref,
    conv_shared_ref,
    conv_shared_bias_ref,
    skip_ref,
    gated_gain_ref,
    w_out_ref,
    next_gain_ref,
    w_next_ref,
    new_ref,
    next_ref,
    kept_ref,
    kept_inner_ref,
    kept_shared_ref,
    gather_buf,
    small_out,
    small_buf,
    square_out,
    square_buf,
    part_out,
    part_buf,
    new_buf,
    message,
    state_out,
    state_pool,
    state_lists,
    state_passing,
    state_final,
    state_second,
    news_pool,
    news_lists,
    news_passing,
    news_final,
    news_second,
    send_sem,
    recv_sem,
    route_send,
    route_recv,
):
    me = lax.axis_index("narrow")
    states = Route(
        0,
        table_ref,
        (state_pool, state_lists, state_passing, state_final, state_second),
        route_send,
        route_recv,
        side,
    )
    updates = Route(
        1,
        table_ref,
        (news_pool, news_lists, news_passing, news_final, news_second),
        route_send,
        route_recv,
        side,
    )
    tokens, block = hidden_ref.shape
    requests = start_ref.shape[0]
    length = tokens // requests
    width = block * count
    barrier = pltpu.get_barrier_semaphore()
    for step in range(1, count):
        pl.semaphore_signal(
            barrier, inc=1, device_id={"narrow": lax.rem(me + step, count)}, device_id_type=MESH
        )
    for half in (0, 1):
        for back in (0, 1):
            pl.semaphore_signal(
                barrier,
                inc=1,
                device_id={"wide": states.neighbour(half, back, 0)},
                device_id_type=MESH,
            )
    pl.semaphore_wait(barrier, count + 3)

    def send(source, target_buf, stage, step):
        pltpu.make_async_remote_copy(
            src_ref=source,
            dst_ref=target_buf.at[me],
            send_sem=send_sem.at[stage],
            recv_sem=recv_sem.at[stage],
            device_id={"narrow": lax.rem(me + step, count)},
            device_id_type=MESH,
        ).start()

    def finish(target_buf, stage):
        some = target_buf.at[pl.ds(0, count - 1)]
        both = pltpu.make_async_remote_copy(
            src_ref=some,
            dst_ref=some,
            send_sem=send_sem.at[stage],
            recv_sem=recv_sem.at[stage],
            device_id={"narrow": lax.rem(me + 1, count)},
            device_id_type=MESH,
        )
        both.wait_recv()
        both.wait_send()

    for step in range(1, count):
        send(hidden_ref, gather_buf, 0, step)
    gather_buf[me] = hidden_ref[...]
    half_rows = start_ref.shape[1] // 2
    states.fill(start_ref, half_rows)
    states.first(0)

    rows = lax.broadcasted_iota(jnp.int32, (tokens, tokens), 0)
    cols = lax.broadcasted_iota(jnp.int32, (tokens, tokens), 1)
    same = (rows >> 4) == (cols >> 4)
    tri = same & (cols <= rows)
    eye = rows == cols
    place = rows[:, :1] & (length - 1)
    acc = acc_ref[...]
    lane = lax.broadcasted_iota(jnp.int32, (tokens, block), 1)

    def to_row(column):
        return jnp.sum(jnp.where(eye, column, 0.0), axis=0, keepdims=True)

    def to_column(row):
        return jnp.sum(jnp.where(eye, row, 0.0), axis=1, keepdims=True)

    def spread(values):
        return jnp.where(
            lane < 64, values[:, 0:1], jnp.where(lane < 128, values[:, 1:2], values[:, 2:3])
        )

    def normed(buf, gains):
        total = jnp.zeros((tokens, 1), F32)
        for n in range(count):
            piece = buf[n].astype(F32)
            total = total + jnp.sum(piece * piece, axis=1, keepdims=True)
        factor = lax.rsqrt(total / width + EPSILON)
        return [(buf[n].astype(F32) * factor * gains[n]).astype(BF16) for n in range(count)]

    states.first(1)
    finish(gather_buf, 0)
    gate = jnp.zeros((tokens, block), F32)
    inner = jnp.zeros((tokens, block), F32)
    small = jnp.zeros((tokens, 128), F32)
    pieces = normed(gather_buf, gain_ref)
    for n in range(count):
        small = small + bdot(pieces[n], w_small_ref[n])
    small_out[...] = small.astype(BF16)
    for step in range(1, count):
        send(small_out, small_buf, 1, step)
    small_buf[me] = small_out[...]
    for n in range(count):
        inner = inner + bdot(pieces[n], w_inner_ref[n])
        gate = gate + bdot(pieces[n], w_gate_ref[n])
    gate = gate.astype(BF16).astype(F32)
    states.first(2)
    inner_bf = inner.astype(BF16)

    def filtered(fresh, tail, weight, offset):
        total = offset + fresh * weight[3:4]
        for shift in (1, 2, 3):
            moved = jnp.where(
                place >= shift,
                pltpu.roll(fresh, shift, 0),
                pltpu.roll(tail, tokens - length + shift, 0),
            )
            total = total + moved * weight[3 - shift : 4 - shift]
        return jax.nn.silu(total)

    tail_inner = tail_inner_ref[...]
    tail_shared = tail_shared_ref[...]
    conv_i = filtered(
        inner_bf.astype(F32),
        tail_inner.astype(F32),
        conv_inner_ref[...].astype(F32),
        conv_inner_bias_ref[...],
    )

    raw = small.astype(BF16).astype(F32) + bias_ref[...]
    steps = jnp.maximum(raw, 0.0) + jnp.log1p(jnp.exp(-jnp.abs(raw)))
    log_decay = steps * -jnp.exp(decay_ref[...])
    cumul = fdot(tri.astype(F32), log_decay)
    col_place = cols & (length - 1)
    ending = fdot((same & (col_place < acc)).astype(F32), log_decay)
    before = place < acc
    factor = jnp.where(before, jnp.exp(jnp.where(before, ending - cumul, 0.0)), 0.0) * steps
    decayed = jnp.exp(ending)
    weighted = (conv_i * spread(factor)).astype(BF16)

    states.first(3)
    finish(small_buf, 1)
    lane_in = lax.broadcasted_iota(jnp.int32, (128, 256), 0)
    lane_out = lax.broadcasted_iota(jnp.int32, (128, 256), 1)
    shared = jnp.zeros((tokens, 256), F32)
    for n in range(count):
        pick = (lane_in >= 32) & (lane_in < 64) & (lane_out == lane_in - 32 + 32 * n)
        shared = shared + bdot(small_buf[n], pick.astype(BF16))
    conv_s = filtered(
        shared, tail_shared.astype(F32), conv_shared_ref[...].astype(F32), conv_shared_bias_ref[...]
    )
    b_part = conv_s[:, :128]
    c_part = conv_s[:, 128:]

    edge = rows[:, :1] & 15
    wanted = jnp.where(
        edge < 3, edge, jnp.where(edge < 6, edge - 3, jnp.where(edge < 9, edge - 6, edge - 9))
    )
    target = acc + wanted - 3
    sel_fresh = (same & (col_place == target)).astype(BF16)
    sel_tail = (same & (col_place == target + length)).astype(BF16)
    edge_i = bdot(sel_fresh, inner_bf) + bdot(sel_tail, tail_inner)
    edge_s = bdot(sel_fresh, shared.astype(BF16)) + bdot(sel_tail, tail_shared)
    pick_in = lax.broadcasted_iota(jnp.int32, (block, 128), 0)
    pick_out = lax.broadcasted_iota(jnp.int32, (block, 128), 1)
    last_head = (pick_in == pick_out + 128).astype(BF16)
    high = decayed.astype(BF16).astype(F32)
    low = decayed - high
    edges = jnp.where(
        edge < 3,
        edge_i[:, :128],
        jnp.where(
            edge < 6,
            bdot(edge_i.astype(BF16), last_head),
            jnp.where(
                edge < 9,
                edge_s[:, :128],
                jnp.where(
                    edge < 12, edge_s[:, 128:], jnp.where(edge == 12, high, jnp.where(edge == 13, low, 0.0))
                ),
            ),
        ),
    )
    message[:, 0:16, :] = weighted[:, :128].reshape(requests, length, 128)
    message[:, 16:32, :] = bdot(weighted, last_head).astype(BF16).reshape(requests, length, 128)
    message[:, 32:48, :] = b_part.astype(BF16).reshape(requests, length, 128)
    message[:, 48:64, :] = edges.astype(BF16).reshape(requests, length, 128)

    updates.fill(message, 32)
    updates.first(0)
    states.first(4)
    states.after(0)

    crossing = lax.dot_general(
        c_part, b_part, (((1,), (1,)), ((), ())), precision=HIGHEST, preferred_element_type=F32
    )
    direct = jnp.zeros((tokens, block), F32)
    for head in range(3):
        column = cumul[:, head : head + 1]
        gap = jnp.where(tri, column - to_row(column), 0.0)
        mixing = jnp.where(tri, jnp.exp(gap), 0.0) * to_row(steps[:, head : head + 1]) * crossing
        direct = direct + fdot(mixing, jnp.where((lane >> 6) == head, conv_i, 0.0))
    updates.first(1)
    states.after(1)
    carried = lax.dot_general(
        c_part.reshape(requests, length, 128),
        start_ref[...].astype(F32),
        (((2,), (2,)), ((0,), (0,))),
        precision=HIGHEST,
        preferred_element_type=F32,
    ).reshape(tokens, block)
    outputs = carried * spread(jnp.exp(cumul)) + direct + skip_ref[...] * conv_i
    gated = outputs * jax.nn.silu(gate)
    square_out[...] = lax.dot_general(
        jnp.ones((8, block), F32),
        gated * gated,
        (((1,), (1,)), ((), ())),
        precision=HIGHEST,
        preferred_element_type=F32,
    )
    for step in range(1, count):
        send(square_out, square_buf, 2, step)
    square_buf[me] = square_out[...]
    scaled = (gated * gated_gain_ref[...]).astype(BF16)
    for step in range(1, count):
        towards = lax.rem(me + step, count)
        part_out[towards] = bdot(scaled, w_out_ref[towards]).astype(BF16)
        send(part_out.at[towards], part_buf, 3, step)
    part_buf[me] = bdot(scaled, w_out_ref[me]).astype(BF16)

    updates.first(2)
    states.after(2)
    finish(square_buf, 2)
    squares = square_buf[0]
    for n in range(1, count):
        squares = squares + square_buf[n]
    factor_out = lax.rsqrt(to_column(squares[0:1]) / width + EPSILON)
    finish(part_buf, 3)
    summed = part_buf[0].astype(F32)
    for n in range(1, count):
        summed = summed + part_buf[n].astype(F32)
    new_ref[...] = (hidden_ref[...].astype(F32) + summed * factor_out).astype(BF16)
    for step in range(1, count):
        send(new_ref, new_buf, 4, step)
    new_buf[me] = new_ref[...]
    updates.first(3)
    states.after(3)
    finish(new_buf, 4)
    pieces = normed(new_buf, next_gain_ref)
    projected = jnp.zeros(next_ref.shape, F32)
    for n in range(count):
        projected = projected + bdot(pieces[n], w_next_ref[n])
    next_ref[...] = projected.astype(BF16)
    updates.first(4)
    updates.after(0)
    updates.after(1)
    updates.after(2)
    updates.after(3)
    states.after(4)
    updates.after(4)
    states.drain()
    updates.drain()
    states.collect(state_out, half_rows)
    updates.collect(message, 32)
    over = (((1,), (1,)), ((0,), (0,)))
    b_rows = message[:, 32:48, :]
    first = lax.dot_general(message[:, 0:16, :], b_rows, over, preferred_element_type=F32)
    last = lax.dot_general(message[:, 16:32, :], b_rows, over, preferred_element_type=F32)
    edges = message[:, 48:64, :].astype(F32)
    kept_inner_ref[:, :, 0:128] = edges[:, 0:3, :].astype(BF16)
    kept_inner_ref[:, :, 128:192] = edges[:, 3:6, 0:64].astype(BF16)
    kept_shared_ref[:, :, 0:128] = edges[:, 6:9, :].astype(BF16)
    kept_shared_ref[:, :, 128:256] = edges[:, 9:12, :].astype(BF16)
    decay = edges[:, 12:13, :] + edges[:, 13:14, :]
    for head in range(3):
        low = 64 * head
        added = first[:, low : low + 64, :] if head < 2 else last[:, 0:64, :]
        kept_ref[:, low : low + 64, :] = (
            state_out[:, low : low + 64, :].astype(F32) * decay[:, :, head : head + 1] + added
        ).astype(BF16)


def whole(memory_space=pltpu.VMEM):
    return pl.BlockSpec(memory_space=memory_space)


def local(
    count,
    hidden,
    start_state,
    tail_inner,
    tail_shared,
    input_gain,
    w_gate_inner,
    w_shared,
    w_step,
    step_bias,
    decay_log,
    conv_inner,
    conv_inner_bias,
    conv_shared,
    conv_shared_bias,
    skip_gain,
    gated_gain,
    w_output,
    next_gain,
    w_next,
    dealing,
    accepted,
    owners,
):
    tokens, block = hidden.shape
    requests, heads, head_size, states = start_state.shape
    length = tokens // requests
    start = start_state.reshape(requests, heads * head_size, states)
    table, accepted_rows = pl.pallas_call(
        table_kernel,
        out_shape=(
            jax.ShapeDtypeStruct((8, 128), jnp.int32),
            jax.ShapeDtypeStruct((tokens, 1), jnp.int32),
        ),
        in_specs=[whole()] * 3,
        out_specs=(whole(), whole()),
        scratch_shapes=[pltpu.VMEM((dealing.shape[0], 8), F32)],
    )(dealing[None, :], owners[None, :], accepted[None, :])

    def pad_tail(tail):
        kept_rows = tail.shape[1]
        return jnp.pad(tail, ((0, 0), (length - kept_rows, 0), (0, 0))).reshape(
            tokens, tail.shape[2]
        )

    def lanes(row):
        return jnp.pad(row, (0, 128 - row.shape[0]))[None, :]

    w_gate = w_gate_inner[:, :block].reshape(count, block, block)
    w_inner = w_gate_inner[:, block:].reshape(count, block, block)
    w_small = jnp.concatenate(
        [
            w_step,
            jnp.zeros((w_step.shape[0], 32 - heads), BF16),
            w_shared,
            jnp.zeros((w_step.shape[0], 64), BF16),
        ],
        axis=1,
    ).reshape(count, block, 128)
    w_out = w_output.reshape(block, count, block).transpose(1, 0, 2)
    routed = []
    for rows in (heads * head_size // 2, 32):
        routed += [
            pltpu.VMEM((2, 112, rows, 128), BF16),
            pltpu.VMEM((2, 2, 16, rows, 128), BF16),
            pltpu.VMEM((2, 2, 32, rows, 128), BF16),
            pltpu.VMEM((2, 32, rows, 128), BF16),
            pltpu.VMEM((2, 2, 48, rows, 128), BF16),
        ]
    new_part, next_input, kept, kept_inner, kept_shared = pl.pallas_call(
        functools.partial(layer_kernel, count, SIDE),
        out_shape=(
            jax.ShapeDtypeStruct((tokens, block), BF16),
            jax.ShapeDtypeStruct((tokens, w_next.shape[1]), BF16),
            jax.ShapeDtypeStruct(start.shape, BF16),
            jax.ShapeDtypeStruct(tail_inner.shape, BF16),
            jax.ShapeDtypeStruct(tail_shared.shape, BF16),
        ),
        in_specs=[whole(pltpu.SMEM)] + [whole()] * 20,
        out_specs=(whole(),) * 5,
        scratch_shapes=[
            pltpu.VMEM((count, tokens, block), BF16),
            pltpu.VMEM((tokens, 128), BF16),
            pltpu.VMEM((count, tokens, 128), BF16),
            pltpu.VMEM((8, tokens), F32),
            pltpu.VMEM((count, 8, tokens), F32),
            pltpu.VMEM((count, tokens, block), BF16),
            pltpu.VMEM((count, tokens, block), BF16),
            pltpu.VMEM((count, tokens, block), BF16),
            pltpu.VMEM((requests, 64, 128), BF16),
            pltpu.VMEM(start.shape, BF16),
            *routed,
            pltpu.SemaphoreType.DMA((5,)),
            pltpu.SemaphoreType.DMA((5,)),
            pltpu.SemaphoreType.DMA((64,)),
            pltpu.SemaphoreType.DMA((64,)),
        ],
        compiler_params=pltpu.CompilerParams(
            collective_id=0, has_side_effects=True, vmem_limit_bytes=58 << 20
        ),
        cost_estimate=pl.CostEstimate(
            flops=4_000_000_000, bytes_accessed=100_000_000, transcendentals=0
        ),
    )(
        table,
        accepted_rows,
        hidden,
        start,
        pad_tail(tail_inner),
        pad_tail(tail_shared),
        input_gain.reshape(count, 1, block),
        w_gate,
        w_inner,
        w_small,
        lanes(step_bias),
        lanes(decay_log),
        conv_inner,
        conv_inner_bias[None, :],
        conv_shared,
        conv_shared_bias[None, :],
        jnp.repeat(skip_gain, head_size)[None, :],
        gated_gain[None, :],
        w_out,
        next_gain.reshape(count, 1, block),
        w_next.reshape(count, block, w_next.shape[1]),
    )
    return (new_part, next_input, kept.reshape(start_state.shape), kept_inner, kept_shared)


def solution(mesh):
    placed = (
        P("wide", "narrow"),
        P("wide", "narrow", None, None),
        P("wide", None, "narrow"),
        P("wide", None, None),
        P(),
        P(None, "narrow"),
        P(None, "narrow"),
        P(None, "narrow"),
        P("narrow"),
        P("narrow"),
        P(None, "narrow"),
        P("narrow"),
        P(),
        P(),
        P("narrow"),
        P("narrow"),
        P("narrow", None),
        P(),
        P(None, "narrow"),
        P(),
        P(),
        P(),
    )
    return jax.shard_map(
        functools.partial(local, mesh.shape["narrow"]),
        mesh=mesh,
        in_specs=placed,
        out_specs=(
            P("wide", "narrow"),
            P("wide", "narrow"),
            P("wide", "narrow", None, None),
            P("wide", None, "narrow"),
            P("wide", None, None),
        ),
        check_vma=False,
    )
```

```python
import functools

import jax
import jax.numpy as jnp
from jax import lax
from jax.experimental import pallas as pl
from jax.experimental.pallas import tpu as pltpu
from jax.sharding import PartitionSpec as P

EPSILON = 1e-05
HIGHEST = lax.Precision.HIGHEST
MESH = pl.DeviceIdType.MESH
F32 = jnp.float32
BF16 = jnp.bfloat16


def fdot(a, b):
    return jnp.dot(a, b, precision=HIGHEST, preferred_element_type=F32)


def bdot(a, b):
    return jnp.dot(a, b, preferred_element_type=F32)


SIDE = 8
FAR = 4
BASE = (0, 0, 16, 32, 44)
STEPS = (4, 12, 16, 16)


def hop_base(dist):
    return jnp.where(dist <= 1, 0, jnp.where(dist == 2, 16, jnp.where(dist == 3, 32, 44)))


def table_values(dealing, owners, accepted, me, per=16):
    T = dealing.shape[1]
    ln = lax.broadcasted_iota(jnp.int32, (1, T), 1)
    sub = lax.broadcasted_iota(jnp.int32, (T, T), 0)
    pick = (sub == dealing).astype(BF16)
    row8 = lax.broadcasted_iota(jnp.int32, (8, T), 0)
    known = jnp.where(row8 == 0, owners, accepted).astype(F32).astype(BF16)
    per_slot = jnp.dot(known, pick, preferred_element_type=F32).astype(jnp.int32)
    owner = per_slot[0:1]
    acc = per_slot[1:2]
    sender = ln >> 4
    ys, zs = sender >> 3, sender & 7
    yo, zo = owner >> 3, owner & 7
    me_y, me_z = me // SIDE, lax.rem(me, SIDE)
    halves = []
    keys, starts = [], []
    for fs, fo, gs, go in ((zs, zo, ys, yo), (ys, yo, zs, zo)):
        d1 = (fo - fs) & 7
        back1 = jnp.where((d1 > FAR) | ((d1 == FAR) & ((go & 1) == 1)), 1, 0)
        dist1 = jnp.where(back1 == 1, SIDE - d1, d1)
        d2 = (go - gs) & 7
        back2 = jnp.where((d2 > FAR) | ((d2 == FAR) & ((fs & 1) == 1)), 1, 0)
        dist2 = jnp.where(back2 == 1, SIDE - d2, d2)
        for group, dist in ((sender * 2 + back1, dist1), (owner * 2 + back2, dist2)):
            start = group * (8 * T)
            starts.append(start.astype(F32))
            keys.append((start + (FAR - dist) * T + ln).astype(F32))
        halves.append((back1, dist1, back2, dist2))
    starts.append((owner * T).astype(F32))
    keys.append((owner * T + dealing).astype(F32))
    stacked = jnp.where(row8 == 0, keys[0], jnp.where(row8 == 1, keys[1], jnp.where(row8 == 2, keys[2], jnp.where(row8 == 3, keys[3], keys[4]))))
    return ln, sender, owner, acc, me_y, me_z, halves, keys, starts, stacked


def finish_tables(ln, sender, owner, acc, me, halves, places):
    T = ln.shape[1]
    lane = lax.broadcasted_iota(jnp.int32, (128, 128), 1)
    sub = lax.broadcasted_iota(jnp.int32, (128, 128), 0)
    t = lax.broadcasted_iota(jnp.int32, (128, 1), 0)
    def to_row(column):
        return jnp.sum(jnp.where(lane == sub, column.astype(F32), 0.0), axis=0, keepdims=True).astype(jnp.int32)
    def lookup(want, key, value, missing):
        return to_row(jnp.max(jnp.where(want == key, value, missing).astype(F32), axis=1, keepdims=True))
    me_y, me_z = me // SIDE, lax.rem(me, SIDE)
    out = []
    for h in (0, 1):
        back1, dist1, back2, dist2 = halves[h]
        pos1, pos2 = places[2 * h], places[2 * h + 1]
        loc = jnp.where(
            dist1 == 0, ln & 15, jnp.minimum(16 + back1 * 48 + hop_base(dist1) + pos1, 111)
        )
        out.append(lookup(me * 32 + t, sender * 32 + back1 * 16 + pos1, ln & 15, 0))
        back_t = jnp.where(t >= 48, 1, 0)
        q = t - 48 * back_t
        hop = jnp.where(q < 4, 4, jnp.where(q < 16, 3, jnp.where(q < 32, 2, 1)))
        i = q - jnp.where(q < 4, 0, jnp.where(q < 16, 4, jnp.where(q < 32, 16, 32)))
        move = jnp.where(back_t == 1, -hop, hop)
        if h == 0:
            dest = ((me_y + move) & 7) * SIDE + me_z
        else:
            dest = me_y * SIDE + ((me_z + move) & 7)
        out.append(lookup(((dest * 2 + back_t) * 8 + hop) * 16 + i, ((owner * 2 + back2) * 8 + dist2) * 16 + pos2, loc, -1))
        out.append(lookup(me * 16 + t, owner * 16 + places[4], jnp.where(dist2 == 0, loc, 128 + jnp.minimum(back2 * 16 + pos2, 31)), 0))
    out.append(lookup(me * 16 + t, ln, acc, 0))
    out.append(out[-1])
    r = lax.broadcasted_iota(jnp.int32, (8, 128), 0)
    table = jnp.zeros((8, 128), jnp.int32)
    for k in range(7):
        table = jnp.where(r == k, out[k], table)
    return table


def table_kernel(dealing_ref, owners_ref, accepted_ref, table_ref, count_ref, columns):
    me = lax.axis_index("wide")
    ln, sender, owner, acc, me_y, me_z, halves, keys, starts, stacked = table_values(
        dealing_ref[...], owners_ref[...], accepted_ref[...], me
    )
    columns[...] = jnp.transpose(stacked)
    total = ln.shape[1]
    chunk = 64

    def count(step, found):
        part = columns[pl.ds(pl.multiple_of(step * chunk, chunk), chunk), :]
        return tuple(
            found[k]
            + jnp.sum(
                jnp.where((part[:, k : k + 1] >= starts[k]) & (part[:, k : k + 1] < keys[k]), 1.0, 0.0),
                axis=0,
                keepdims=True,
            )
            for k in range(5)
        )

    found = lax.fori_loop(
        0, total // chunk, count, tuple(jnp.zeros((1, total), F32) for _ in range(5))
    )
    table_ref[...] = finish_tables(
        ln, sender, owner, acc, me, halves, [places.astype(jnp.int32) for places in found]
    )
    tokens = count_ref.shape[0]
    slot = lax.broadcasted_iota(jnp.int32, (tokens, total), 0) >> 4
    at = lax.broadcasted_iota(jnp.int32, (tokens, total), 1)
    count_ref[...] = jnp.sum(
        jnp.where(at == me * 16 + slot, acc, 0).astype(F32), axis=1, keepdims=True
    ).astype(jnp.int32)


CAPS = (16, 16, 12, 4)
OFFS = (0, 16, 32, 44)
SECOND_OFFS = (0, 4, 16, 32)


class Route:
    def __init__(self, number, table, refs, send_sem, recv_sem, side):
        self.number, self.table = number, table
        self.send_sem, self.recv_sem, self.side = send_sem, recv_sem, side
        self.pool, self.lists, self.passing, self.final, self.second = refs

    def neighbour(self, half, back, phase):
        me = lax.axis_index("wide")
        side = self.side
        y, z = me // side, lax.rem(me, side)
        move = side - 1 if back else 1
        if (half == 0) == (phase == 0):
            return y * side + lax.rem(z + move, side)
        return lax.rem(y + move, side) * side + z

    def copy(self, phase, half, back, hop):
        if phase == 0:
            low = 16 + 48 * back
            if hop == 0:
                source = self.lists.at[half, back]
            else:
                source = self.pool.at[half, pl.ds(low + OFFS[hop - 1], CAPS[hop])]
            target = self.pool.at[half, pl.ds(low + OFFS[hop], CAPS[hop])]
        else:
            size = CAPS[3 - hop]
            source = self.second.at[half, back, pl.ds(SECOND_OFFS[hop], size)]
            if hop < 3:
                target = self.passing.at[half, back, pl.ds(SECOND_OFFS[hop], size)]
            else:
                target = self.final.at[half, pl.ds(16 * back, size)]
        at = (((self.number * 2 + phase) * 2 + half) * 2 + back) * 4 + hop
        return pltpu.make_async_remote_copy(
            src_ref=source,
            dst_ref=target,
            send_sem=self.send_sem.at[at],
            recv_sem=self.recv_sem.at[at],
            device_id={"wide": self.neighbour(half, back, phase)},
            device_id_type=MESH,
        )

    def each(self, phase, hop):
        return [self.copy(phase, half, back, hop) for half in (0, 1) for back in (0, 1)]

    def fill(self, blocks, rows):
        for half in (0, 1):
            low = half * rows

            def own(i, carry):
                self.pool[half, i] = blocks[i, low : low + rows, :]
                return carry

            lax.fori_loop(0, 16, own, 0)
            for back in (0, 1):

                def listed(i, carry):
                    self.lists[half, back, i] = blocks[jnp.clip(self.table[3 * half, 16 * back + i], 0, 15), low : low + rows, :]
                    return carry

                lax.fori_loop(0, 16, listed, 0)

    def first(self, hop):
        if hop > 0:
            for copy in self.each(0, hop - 1):
                copy.wait_recv()
        if hop < 4:
            for copy in self.each(0, hop):
                copy.start()

    def after(self, hop):
        if hop > 0:
            for copy in self.each(1, hop - 1):
                copy.wait_recv()
        if hop == 4:
            return
        low = SECOND_OFFS[hop]
        size = CAPS[3 - hop]
        known = CAPS[4 - hop] if hop > 0 else 0
        for half in (0, 1):
            for back in (0, 1):

                def merged(i, carry):
                    at = self.table[3 * half + 1, 48 * back + low + i]
                    mine = self.pool[half, jnp.clip(at, 0, 111)]
                    came = self.passing[half, back, SECOND_OFFS[hop - 1] + i]
                    self.second[half, back, low + i] = jnp.where(at >= 0, mine, came)
                    return carry

                def fresh(i, carry):
                    at = self.table[3 * half + 1, 48 * back + low + i]
                    self.second[half, back, low + i] = self.pool[half, jnp.clip(at, 0, 111)]
                    return carry

                if known:
                    lax.fori_loop(0, known, merged, 0)
                if known < size:
                    lax.fori_loop(known, size, fresh, 0)
        for copy in self.each(1, hop):
            copy.start()

    def collect(self, blocks, rows):
        for half in (0, 1):
            low = half * rows

            def take(k, carry):
                at = self.table[3 * half + 2, k]
                here = self.pool[half, jnp.clip(jnp.where(at < 128, at, 0), 0, 111)]
                came = self.final[half, jnp.clip(at - 128, 0, 31)]
                blocks[k, low : low + rows, :] = jnp.where(at < 128, here, came)
                return carry

            lax.fori_loop(0, 16, take, 0)

    def drain(self):
        for phase in (0, 1):
            for hop in range(4):
                for copy in self.each(phase, hop):
                    copy.wait_send()


def layer_kernel(
    count,
    side,
    table_ref,
    bias_ref,
    decay_ref,
    skip_ref,
    acc_ref,
    hidden_ref,
    start_ref,
    tail_inner_ref,
    tail_shared_ref,
    gain_ref,
    w_gate_inner_ref,
    w_shared_ref,
    w_step_ref,
    conv_inner_ref,
    conv_inner_bias_ref,
    conv_shared_ref,
    conv_shared_bias_ref,
    gated_gain_ref,
    w_out_ref,
    next_gain_ref,
    w_next_ref,
    new_ref,
    next_ref,
    kept_ref,
    kept_inner_ref,
    kept_shared_ref,
    gather_buf,
    small_out,
    small_buf,
    square_out,
    square_buf,
    part_out,
    part_buf,
    new_buf,
    stack,
    message,
    state_out,
    state_pool,
    state_lists,
    state_passing,
    state_final,
    state_second,
    news_pool,
    news_lists,
    news_passing,
    news_final,
    news_second,
    send_sem,
    recv_sem,
    route_send,
    route_recv,
):
    me = lax.axis_index("narrow")
    states = Route(
        0,
        table_ref,
        (state_pool, state_lists, state_passing, state_final, state_second),
        route_send,
        route_recv,
        side,
    )
    updates = Route(
        1,
        table_ref,
        (news_pool, news_lists, news_passing, news_final, news_second),
        route_send,
        route_recv,
        side,
    )
    block, tokens = hidden_ref.shape
    requests = start_ref.shape[0]
    length = tokens // requests
    width = block * count
    barrier = pltpu.get_barrier_semaphore()
    for step in range(1, count):
        pl.semaphore_signal(
            barrier, inc=1, device_id={"narrow": lax.rem(me + step, count)}, device_id_type=MESH
        )
    for half in (0, 1):
        for back in (0, 1):
            pl.semaphore_signal(
                barrier,
                inc=1,
                device_id={"wide": states.neighbour(half, back, 0)},
                device_id_type=MESH,
            )
    pl.semaphore_wait(barrier, count + 3)

    def send(source, target_buf, stage, step):
        pltpu.make_async_remote_copy(
            src_ref=source,
            dst_ref=target_buf.at[me],
            send_sem=send_sem.at[stage],
            recv_sem=recv_sem.at[stage],
            device_id={"narrow": lax.rem(me + step, count)},
            device_id_type=MESH,
        ).start()

    def finish(target_buf, stage):
        some = target_buf.at[pl.ds(0, count - 1)]
        both = pltpu.make_async_remote_copy(
            src_ref=some,
            dst_ref=some,
            send_sem=send_sem.at[stage],
            recv_sem=recv_sem.at[stage],
            device_id={"narrow": lax.rem(me + 1, count)},
            device_id_type=MESH,
        )
        both.wait_recv()
        both.wait_send()

    for step in range(1, count):
        send(hidden_ref, gather_buf, 0, step)
    gather_buf[me] = hidden_ref[...]
    half_rows = start_ref.shape[1] // 2
    states.fill(start_ref, half_rows)
    states.first(0)

    rows = lax.broadcasted_iota(jnp.int32, (tokens, tokens), 0)
    cols = lax.broadcasted_iota(jnp.int32, (tokens, tokens), 1)
    same = (rows >> 4) == (cols >> 4)
    tri = same & (cols <= rows)
    eye = rows == cols
    place = rows[:, :1] & (length - 1)
    acc = acc_ref[...]
    lane = lax.broadcasted_iota(jnp.int32, (tokens, block), 1)
    small_eye = lax.broadcasted_iota(jnp.int32, (block, block), 0) == lax.broadcasted_iota(
        jnp.int32, (block, block), 1
    )
    turn = small_eye.astype(BF16)

    def to_row(column):
        return jnp.sum(jnp.where(eye, column, 0.0), axis=0, keepdims=True)

    def gain_column(gains, n):
        return jnp.sum(
            jnp.where(small_eye, gains[:, n * block : (n + 1) * block], 0.0), axis=1, keepdims=True
        )

    def spread(values):
        return jnp.where(
            lane < 64, values[:, 0:1], jnp.where(lane < 128, values[:, 1:2], values[:, 2:3])
        )

    def scalars(ref, where, limit):
        return jnp.where(where < limit, ref[0], jnp.where(where < 2 * limit, ref[1], ref[2]))

    def normed(buf, gains):
        total = jnp.zeros((1, tokens), F32)
        for n in range(count):
            piece = buf[n].astype(F32)
            total = total + jnp.sum(piece * piece, axis=0, keepdims=True)
        factor = lax.rsqrt(total / width + EPSILON)
        for n in range(count):
            stack[n * block : (n + 1) * block, :] = (
                buf[n].astype(F32) * factor * gains[n]
            ).astype(BF16)

    gains_now = gain_ref[...].reshape(1, width)
    gains_now = [gain_column(gains_now, n) for n in range(count)]
    states.first(1)
    finish(gather_buf, 0)
    normed(gather_buf, gains_now)
    upright = (((0,), (0,)), ((), ()))
    small_out[...] = bdot(w_shared_ref[...], stack[...]).astype(BF16)
    for step in range(1, count):
        send(small_out, small_buf, 1, step)
    small_buf[me] = small_out[...]
    step_raw = bdot(w_step_ref[...], stack[...]).astype(BF16)
    both = lax.dot_general(
        w_gate_inner_ref[...], stack[...], upright, preferred_element_type=F32
    ).astype(BF16)
    gate = lax.dot_general(both[:block], turn, upright, preferred_element_type=F32)
    inner_bf = lax.dot_general(both[block:], turn, upright, preferred_element_type=F32).astype(BF16)
    states.first(2)

    def filtered(fresh, tail, weight, offset):
        total = offset + fresh * weight[3:4]
        for shift in (1, 2, 3):
            moved = jnp.where(
                place >= shift,
                pltpu.roll(fresh, shift, 0),
                pltpu.roll(tail, tokens - length + shift, 0),
            )
            total = total + moved * weight[3 - shift : 4 - shift]
        return jax.nn.silu(total)

    def padded(ref):
        total = jnp.zeros((tokens, ref.shape[2]), F32)
        at = lax.broadcasted_iota(jnp.int32, (tokens, requests), 0)
        slot = lax.broadcasted_iota(jnp.int32, (tokens, requests), 1)
        kept_rows = ref.shape[0]
        for q in range(kept_rows):
            put = ((at >> 4) == slot) & ((at & (length - 1)) == length - kept_rows + q)
            total = total + bdot(put.astype(BF16), ref[q])
        return total.astype(BF16)

    tail_inner = padded(tail_inner_ref)
    tail_shared = padded(tail_shared_ref)
    conv_i = filtered(
        inner_bf.astype(F32),
        tail_inner.astype(F32),
        conv_inner_ref[...].astype(F32),
        conv_inner_bias_ref[...],
    )

    heads = w_step_ref.shape[0]
    head_lane = lax.broadcasted_iota(jnp.int32, (heads, 128), 1)
    head_eye = (head_lane == lax.broadcasted_iota(jnp.int32, (heads, 128), 0)).astype(BF16)
    lane_row = lax.broadcasted_iota(jnp.int32, (1, 128), 1)
    raw = lax.dot_general(step_raw, head_eye, upright, preferred_element_type=F32) + scalars(
        bias_ref, lane_row, 1
    )
    steps = jnp.maximum(raw, 0.0) + jnp.log1p(jnp.exp(-jnp.abs(raw)))
    log_decay = steps * -jnp.exp(scalars(decay_ref, lane_row, 1))
    cumul = fdot(tri.astype(F32), log_decay)
    col_place = cols & (length - 1)
    ending = fdot((same & (col_place < acc)).astype(F32), log_decay)
    before = place < acc
    factor = jnp.where(before, jnp.exp(jnp.where(before, ending - cumul, 0.0)), 0.0) * steps
    decayed = jnp.exp(ending)
    weighted = (conv_i * spread(factor)).astype(BF16)

    states.first(3)
    finish(small_buf, 1)
    shared = lax.dot_general(
        small_buf[...].reshape(tokens, tokens),
        eye.astype(BF16),
        upright,
        preferred_element_type=F32,
    )
    conv_s = filtered(
        shared, tail_shared.astype(F32), conv_shared_ref[...].astype(F32), conv_shared_bias_ref[...]
    )
    b_part = conv_s[:, :128]
    c_part = conv_s[:, 128:]

    edge = rows[:, :1] & 15
    wanted = jnp.where(
        edge < 3, edge, jnp.where(edge < 6, edge - 3, jnp.where(edge < 9, edge - 6, edge - 9))
    )
    target = acc + wanted - 3
    sel_fresh = (same & (col_place == target)).astype(BF16)
    sel_tail = (same & (col_place == target + length)).astype(BF16)
    edge_i = bdot(sel_fresh, inner_bf) + bdot(sel_tail, tail_inner)
    edge_s = bdot(sel_fresh, shared.astype(BF16)) + bdot(sel_tail, tail_shared)
    pick_in = lax.broadcasted_iota(jnp.int32, (block, 128), 0)
    pick_out = lax.broadcasted_iota(jnp.int32, (block, 128), 1)
    last_head = (pick_in == pick_out + 128).astype(BF16)
    high = decayed.astype(BF16).astype(F32)
    low = decayed - high
    edges = jnp.where(
        edge < 3,
        edge_i[:, :128],
        jnp.where(
            edge < 6,
            bdot(edge_i.astype(BF16), last_head),
            jnp.where(
                edge < 9,
                edge_s[:, :128],
                jnp.where(
                    edge < 12, edge_s[:, 128:], jnp.where(edge == 12, high, jnp.where(edge == 13, low, 0.0))
                ),
            ),
        ),
    )
    message[:, 0:16, :] = weighted[:, :128].reshape(requests, length, 128)
    message[:, 16:32, :] = bdot(weighted, last_head).astype(BF16).reshape(requests, length, 128)
    message[:, 32:48, :] = b_part.astype(BF16).reshape(requests, length, 128)
    message[:, 48:64, :] = edges.astype(BF16).reshape(requests, length, 128)

    updates.fill(message, 32)
    updates.first(0)
    states.first(4)
    states.after(0)

    crossing = lax.dot_general(
        c_part, b_part, (((1,), (1,)), ((), ())), precision=HIGHEST, preferred_element_type=F32
    )
    direct = jnp.zeros((tokens, block), F32)
    for head in range(3):
        column = cumul[:, head : head + 1]
        gap = jnp.where(tri, column - to_row(column), 0.0)
        mixing = jnp.where(tri, jnp.exp(gap), 0.0) * to_row(steps[:, head : head + 1]) * crossing
        direct = direct + fdot(mixing, jnp.where((lane >> 6) == head, conv_i, 0.0))
    updates.first(1)
    states.after(1)
    carried = lax.dot_general(
        c_part.reshape(requests, length, 128),
        start_ref[...].astype(F32),
        (((2,), (2,)), ((0,), (0,))),
        precision=HIGHEST,
        preferred_element_type=F32,
    ).reshape(tokens, block)
    outputs = carried * spread(jnp.exp(cumul)) + direct + scalars(skip_ref, lane, 64) * conv_i
    gated = outputs * jax.nn.silu(gate)
    square_out[...] = lax.dot_general(
        jnp.ones((8, block), F32),
        gated * gated,
        (((1,), (1,)), ((), ())),
        precision=HIGHEST,
        preferred_element_type=F32,
    )
    for step in range(1, count):
        send(square_out, square_buf, 2, step)
    square_buf[me] = square_out[...]
    scaled = (gated * gated_gain_ref[...]).astype(BF16)
    scaled = lax.dot_general(
        turn, scaled, (((1,), (1,)), ((), ())), preferred_element_type=F32
    ).astype(BF16)
    part_out[...] = (
        lax.dot_general(w_out_ref[...], scaled, upright, preferred_element_type=F32)
        .astype(BF16)
        .reshape(count, block, tokens)
    )
    for step in range(1, count):
        send(part_out.at[lax.rem(me + step, count)], part_buf, 3, step)
    part_buf[me] = part_out[me]

    updates.first(2)
    states.after(2)
    finish(square_buf, 2)
    squares = square_buf[0]
    for n in range(1, count):
        squares = squares + square_buf[n]
    factor_out = lax.rsqrt(squares[0:1] / width + EPSILON)
    finish(part_buf, 3)
    summed = part_buf[0].astype(F32)
    for n in range(1, count):
        summed = summed + part_buf[n].astype(F32)
    new_ref[...] = (hidden_ref[...].astype(F32) + summed * factor_out).astype(BF16)
    for step in range(1, count):
        send(new_ref, new_buf, 4, step)
    new_buf[me] = new_ref[...]
    updates.first(3)
    states.after(3)
    finish(new_buf, 4)
    gains_next = next_gain_ref[...].reshape(1, width)
    normed(new_buf, [gain_column(gains_next, n) for n in range(count)])
    next_ref[...] = bdot(w_next_ref[...], stack[...]).astype(BF16)
    updates.first(4)
    updates.after(0)
    updates.after(1)
    updates.after(2)
    updates.after(3)
    states.after(4)
    updates.after(4)
    states.drain()
    updates.drain()
    states.collect(state_out, half_rows)
    updates.collect(message, 32)
    over = (((1,), (1,)), ((0,), (0,)))
    b_rows = message[:, 32:48, :]
    first = lax.dot_general(message[:, 0:16, :], b_rows, over, preferred_element_type=F32)
    last = lax.dot_general(message[:, 16:32, :], b_rows, over, preferred_element_type=F32)
    edges = message[:, 48:64, :].astype(F32)
    swap = ((rows >> 4) == (cols & 15)) & ((rows & 15) == (cols >> 4))
    by_row = bdot(swap.astype(BF16), message[:, 48:64, :].reshape(tokens, 128)).astype(BF16)
    for q in range(3):
        kept_inner_ref[q, :, 0:128] = by_row[16 * q : 16 * q + 16]
        kept_inner_ref[q, :, 128:192] = by_row[48 + 16 * q : 64 + 16 * q, 0:64]
        kept_shared_ref[q, :, 0:128] = by_row[96 + 16 * q : 112 + 16 * q]
        kept_shared_ref[q, :, 128:256] = by_row[144 + 16 * q : 160 + 16 * q]
    decay = edges[:, 12:13, :] + edges[:, 13:14, :]
    for head in range(3):
        low = 64 * head
        added = first[:, low : low + 64, :] if head < 2 else last[:, 0:64, :]
        kept_ref[:, low : low + 64, :] = (
            state_out[:, low : low + 64, :].astype(F32) * decay[:, :, head : head + 1] + added
        ).astype(BF16)


def whole(memory_space=pltpu.VMEM):
    return pl.BlockSpec(memory_space=memory_space)


def local(
    count,
    hidden,
    start_state,
    tail_inner,
    tail_shared,
    input_gain,
    w_gate_inner,
    w_shared,
    w_step,
    step_bias,
    decay_log,
    conv_inner,
    conv_inner_bias,
    conv_shared,
    conv_shared_bias,
    skip_gain,
    gated_gain,
    w_output,
    next_gain,
    w_next,
    dealing,
    accepted,
    owners,
):
    tokens, block = hidden.shape
    requests, heads, head_size, states = start_state.shape
    start = start_state.reshape(requests, heads * head_size, states)
    routed = []
    for rows in (heads * head_size // 2, 32):
        routed += [
            pltpu.VMEM((2, 112, rows, 128), BF16),
            pltpu.VMEM((2, 2, 16, rows, 128), BF16),
            pltpu.VMEM((2, 2, 32, rows, 128), BF16),
            pltpu.VMEM((2, 32, rows, 128), BF16),
            pltpu.VMEM((2, 2, 48, rows, 128), BF16),
        ]
    shared_here = w_shared.shape[1]
    table, accepted_rows = pl.pallas_call(
        table_kernel,
        out_shape=(
            jax.ShapeDtypeStruct((8, 128), jnp.int32),
            jax.ShapeDtypeStruct((tokens, 1), jnp.int32),
        ),
        in_specs=[whole()] * 3,
        out_specs=(whole(), whole()),
        scratch_shapes=[pltpu.VMEM((dealing.shape[0], 8), F32)],
    )(dealing[None, :], owners[None, :], accepted[None, :])
    operands = (
        table,
        step_bias,
        decay_log,
        skip_gain,
        accepted_rows,
        hidden.T,
        start,
        tail_inner.transpose(1, 0, 2),
        tail_shared.transpose(1, 0, 2),
        input_gain,
        w_gate_inner,
        w_shared.T,
        w_step.T,
        conv_inner,
        conv_inner_bias[None, :],
        conv_shared,
        conv_shared_bias[None, :],
        gated_gain[None, :],
        w_output,
        next_gain,
        w_next.T,
    )
    blocks = pltpu.VMEM((count, block, tokens), BF16)
    new_part, next_input, kept, kept_inner, kept_shared = pl.pallas_call(
        functools.partial(layer_kernel, count, SIDE),
        out_shape=(
            jax.ShapeDtypeStruct((block, tokens), BF16),
            jax.ShapeDtypeStruct((w_next.shape[1], tokens), BF16),
            jax.ShapeDtypeStruct(start.shape, BF16),
            jax.ShapeDtypeStruct((3, requests, tail_inner.shape[2]), BF16),
            jax.ShapeDtypeStruct((3, requests, tail_shared.shape[2]), BF16),
        ),
        in_specs=[whole(pltpu.SMEM)] * 4 + [whole()] * (len(operands) - 4),
        out_specs=(whole(),) * 5,
        scratch_shapes=[
            blocks,
            pltpu.VMEM((shared_here, tokens), BF16),
            pltpu.VMEM((count, shared_here, tokens), BF16),
            pltpu.VMEM((8, tokens), F32),
            pltpu.VMEM((count, 8, tokens), F32),
            blocks,
            blocks,
            blocks,
            pltpu.VMEM((count * block, tokens), BF16),
            pltpu.VMEM((requests, 64, 128), BF16),
            pltpu.VMEM(start.shape, BF16),
            *routed,
            pltpu.SemaphoreType.DMA((5,)),
            pltpu.SemaphoreType.DMA((5,)),
            pltpu.SemaphoreType.DMA((64,)),
            pltpu.SemaphoreType.DMA((64,)),
        ],
        compiler_params=pltpu.CompilerParams(
            collective_id=0, has_side_effects=True, vmem_limit_bytes=58 << 20
        ),
        cost_estimate=pl.CostEstimate(
            flops=4_000_000_000, bytes_accessed=100_000_000, transcendentals=0
        ),
    )(*operands)
    return (
        new_part.T,
        next_input.T,
        kept.reshape(start_state.shape),
        kept_inner.transpose(1, 0, 2),
        kept_shared.transpose(1, 0, 2),
    )


def solution(mesh):
    placed = (
        P("wide", "narrow"),
        P("wide", "narrow", None, None),
        P("wide", None, "narrow"),
        P("wide", None, None),
        P(),
        P(None, "narrow"),
        P(None, "narrow"),
        P(None, "narrow"),
        P("narrow"),
        P("narrow"),
        P(None, "narrow"),
        P("narrow"),
        P(),
        P(),
        P("narrow"),
        P("narrow"),
        P("narrow", None),
        P(),
        P(None, "narrow"),
        P(),
        P(),
        P(),
    )
    return jax.shard_map(
        functools.partial(local, mesh.shape["narrow"]),
        mesh=mesh,
        in_specs=placed,
        out_specs=(
            P("wide", "narrow"),
            P("wide", "narrow"),
            P("wide", "narrow", None, None),
            P("wide", None, "narrow"),
            P("wide", None, None),
        ),
        check_vma=False,
    )
```

```python
import functools

import jax
import jax.numpy as jnp
from jax import lax
from jax.experimental import pallas as pl
from jax.experimental.pallas import tpu as pltpu
from jax.sharding import PartitionSpec as P

EPSILON = 1e-05
HIGHEST = lax.Precision.HIGHEST
MESH = pl.DeviceIdType.MESH
F32 = jnp.float32
BF16 = jnp.bfloat16


def fdot(a, b):
    return jnp.dot(a, b, precision=HIGHEST, preferred_element_type=F32)


def bdot(a, b):
    return jnp.dot(a, b, preferred_element_type=F32)


SIDE = 8
FAR = 4
BASE = (0, 0, 16, 32, 44)
STEPS = (4, 12, 16, 16)


def hop_base(dist):
    return jnp.where(dist <= 1, 0, jnp.where(dist == 2, 16, jnp.where(dist == 3, 32, 44)))


def table_values(dealing, owners, accepted, me, per=16):
    T = dealing.shape[1]
    ln = lax.broadcasted_iota(jnp.int32, (1, T), 1)
    sub = lax.broadcasted_iota(jnp.int32, (T, T), 0)
    pick = (sub == dealing).astype(BF16)
    row8 = lax.broadcasted_iota(jnp.int32, (8, T), 0)
    known = jnp.where(row8 == 0, owners, accepted).astype(F32).astype(BF16)
    per_slot = jnp.dot(known, pick, preferred_element_type=F32).astype(jnp.int32)
    owner = per_slot[0:1]
    acc = per_slot[1:2]
    sender = ln >> 4
    ys, zs = sender >> 3, sender & 7
    yo, zo = owner >> 3, owner & 7
    me_y, me_z = me // SIDE, lax.rem(me, SIDE)
    halves = []
    keys, starts = [], []
    for fs, fo, gs, go in ((zs, zo, ys, yo), (ys, yo, zs, zo)):
        d1 = (fo - fs) & 7
        back1 = jnp.where((d1 > FAR) | ((d1 == FAR) & ((go & 1) == 1)), 1, 0)
        dist1 = jnp.where(back1 == 1, SIDE - d1, d1)
        d2 = (go - gs) & 7
        back2 = jnp.where((d2 > FAR) | ((d2 == FAR) & ((fs & 1) == 1)), 1, 0)
        dist2 = jnp.where(back2 == 1, SIDE - d2, d2)
        for group, dist in ((sender * 2 + back1, dist1), (owner * 2 + back2, dist2)):
            start = group * (8 * T)
            starts.append(start.astype(F32))
            keys.append((start + (FAR - dist) * T + ln).astype(F32))
        halves.append((back1, dist1, back2, dist2))
    starts.append((owner * T).astype(F32))
    keys.append((owner * T + dealing).astype(F32))
    stacked = jnp.where(row8 == 0, keys[0], jnp.where(row8 == 1, keys[1], jnp.where(row8 == 2, keys[2], jnp.where(row8 == 3, keys[3], keys[4]))))
    return ln, sender, owner, acc, me_y, me_z, halves, keys, starts, stacked


def finish_tables(ln, sender, owner, acc, me, halves, places):
    T = ln.shape[1]
    lane = lax.broadcasted_iota(jnp.int32, (128, 128), 1)
    sub = lax.broadcasted_iota(jnp.int32, (128, 128), 0)
    t = lax.broadcasted_iota(jnp.int32, (128, 1), 0)
    def to_row(column):
        return jnp.sum(jnp.where(lane == sub, column.astype(F32), 0.0), axis=0, keepdims=True).astype(jnp.int32)
    def lookup(want, key, value, missing):
        return to_row(jnp.max(jnp.where(want == key, value, missing).astype(F32), axis=1, keepdims=True))
    me_y, me_z = me // SIDE, lax.rem(me, SIDE)
    out = []
    for h in (0, 1):
        back1, dist1, back2, dist2 = halves[h]
        pos1, pos2 = places[2 * h], places[2 * h + 1]
        loc = jnp.where(
            dist1 == 0, ln & 15, jnp.minimum(16 + back1 * 48 + hop_base(dist1) + pos1, 111)
        )
        out.append(lookup(me * 32 + t, sender * 32 + back1 * 16 + pos1, ln & 15, 0))
        back_t = jnp.where(t >= 48, 1, 0)
        q = t - 48 * back_t
        hop = jnp.where(q < 4, 4, jnp.where(q < 16, 3, jnp.where(q < 32, 2, 1)))
        i = q - jnp.where(q < 4, 0, jnp.where(q < 16, 4, jnp.where(q < 32, 16, 32)))
        move = jnp.where(back_t == 1, -hop, hop)
        if h == 0:
            dest = ((me_y + move) & 7) * SIDE + me_z
        else:
            dest = me_y * SIDE + ((me_z + move) & 7)
        out.append(lookup(((dest * 2 + back_t) * 8 + hop) * 16 + i, ((owner * 2 + back2) * 8 + dist2) * 16 + pos2, loc, -1))
        out.append(lookup(me * 16 + t, owner * 16 + places[4], jnp.where(dist2 == 0, loc, 128 + jnp.minimum(back2 * 16 + pos2, 31)), 0))
    out.append(lookup(me * 16 + t, ln, acc, 0))
    out.append(out[-1])
    r = lax.broadcasted_iota(jnp.int32, (8, 128), 0)
    table = jnp.zeros((8, 128), jnp.int32)
    for k in range(7):
        table = jnp.where(r == k, out[k], table)
    return table


def table_kernel(dealing_ref, owners_ref, accepted_ref, table_ref, count_ref, columns):
    me = lax.axis_index("wide")
    ln, sender, owner, acc, me_y, me_z, halves, keys, starts, stacked = table_values(
        dealing_ref[...], owners_ref[...], accepted_ref[...], me
    )
    columns[...] = jnp.transpose(stacked)
    total = ln.shape[1]
    chunk = 64

    def count(step, found):
        part = columns[pl.ds(pl.multiple_of(step * chunk, chunk), chunk), :]
        return tuple(
            found[k]
            + jnp.sum(
                jnp.where((part[:, k : k + 1] >= starts[k]) & (part[:, k : k + 1] < keys[k]), 1.0, 0.0),
                axis=0,
                keepdims=True,
            )
            for k in range(5)
        )

    found = lax.fori_loop(
        0, total // chunk, count, tuple(jnp.zeros((1, total), F32) for _ in range(5))
    )
    table_ref[...] = finish_tables(
        ln, sender, owner, acc, me, halves, [places.astype(jnp.int32) for places in found]
    )
    tokens = count_ref.shape[0]
    slot = lax.broadcasted_iota(jnp.int32, (tokens, total), 0) >> 4
    at = lax.broadcasted_iota(jnp.int32, (tokens, total), 1)
    count_ref[...] = jnp.sum(
        jnp.where(at == me * 16 + slot, acc, 0).astype(F32), axis=1, keepdims=True
    ).astype(jnp.int32)


CAPS = (16, 16, 12, 4)
OFFS = (0, 16, 32, 44)
SECOND_OFFS = (0, 4, 16, 32)


class Route:
    def __init__(self, number, table, refs, send_sem, recv_sem, side):
        self.number, self.table = number, table
        self.send_sem, self.recv_sem, self.side = send_sem, recv_sem, side
        self.pool, self.lists, self.passing, self.final, self.second = refs

    def neighbour(self, half, back, phase):
        me = lax.axis_index("wide")
        side = self.side
        y, z = me // side, lax.rem(me, side)
        move = side - 1 if back else 1
        if (half == 0) == (phase == 0):
            return y * side + lax.rem(z + move, side)
        return lax.rem(y + move, side) * side + z

    def copy(self, phase, half, back, hop):
        if phase == 0:
            low = 16 + 48 * back
            if hop == 0:
                source = self.lists.at[half, back]
            else:
                source = self.pool.at[half, pl.ds(low + OFFS[hop - 1], CAPS[hop])]
            target = self.pool.at[half, pl.ds(low + OFFS[hop], CAPS[hop])]
        else:
            size = CAPS[3 - hop]
            source = self.second.at[half, back, pl.ds(SECOND_OFFS[hop], size)]
            if hop < 3:
                target = self.passing.at[half, back, pl.ds(SECOND_OFFS[hop], size)]
            else:
                target = self.final.at[half, pl.ds(16 * back, size)]
        at = (((self.number * 2 + phase) * 2 + half) * 2 + back) * 4 + hop
        return pltpu.make_async_remote_copy(
            src_ref=source,
            dst_ref=target,
            send_sem=self.send_sem.at[at],
            recv_sem=self.recv_sem.at[at],
            device_id={"wide": self.neighbour(half, back, phase)},
            device_id_type=MESH,
        )

    def each(self, phase, hop):
        return [self.copy(phase, half, back, hop) for half in (0, 1) for back in (0, 1)]

    def fill(self, blocks, rows):
        for half in (0, 1):
            low = half * rows

            def own(i, carry):
                self.pool[half, i] = blocks[i, low : low + rows, :]
                return carry

            lax.fori_loop(0, 16, own, 0)
            for back in (0, 1):

                def listed(i, carry):
                    self.lists[half, back, i] = blocks[jnp.clip(self.table[3 * half, 16 * back + i], 0, 15), low : low + rows, :]
                    return carry

                lax.fori_loop(0, 16, listed, 0)

    def first(self, hop):
        if hop > 0:
            for copy in self.each(0, hop - 1):
                copy.wait_recv()
        if hop < 4:
            for copy in self.each(0, hop):
                copy.start()

    def after(self, hop):
        if hop > 0:
            for copy in self.each(1, hop - 1):
                copy.wait_recv()
        if hop == 4:
            return
        low = SECOND_OFFS[hop]
        size = CAPS[3 - hop]
        known = CAPS[4 - hop] if hop > 0 else 0
        for half in (0, 1):
            for back in (0, 1):

                def merged(i, carry):
                    at = self.table[3 * half + 1, 48 * back + low + i]
                    mine = self.pool[half, jnp.clip(at, 0, 111)]
                    came = self.passing[half, back, SECOND_OFFS[hop - 1] + i]
                    self.second[half, back, low + i] = jnp.where(at >= 0, mine, came)
                    return carry

                def fresh(i, carry):
                    at = self.table[3 * half + 1, 48 * back + low + i]
                    self.second[half, back, low + i] = self.pool[half, jnp.clip(at, 0, 111)]
                    return carry

                if known:
                    lax.fori_loop(0, known, merged, 0)
                if known < size:
                    lax.fori_loop(known, size, fresh, 0)
        for copy in self.each(1, hop):
            copy.start()

    def collect(self, blocks, rows):
        for half in (0, 1):
            low = half * rows

            def take(k, carry):
                at = self.table[3 * half + 2, k]
                here = self.pool[half, jnp.clip(jnp.where(at < 128, at, 0), 0, 111)]
                came = self.final[half, jnp.clip(at - 128, 0, 31)]
                blocks[k, low : low + rows, :] = jnp.where(at < 128, here, came)
                return carry

            lax.fori_loop(0, 16, take, 0)

    def drain(self):
        for phase in (0, 1):
            for hop in range(4):
                for copy in self.each(phase, hop):
                    copy.wait_send()


def layer_kernel(
    count,
    side,
    table_ref,
    bias_ref,
    decay_ref,
    skip_ref,
    acc_ref,
    hidden_ref,
    start_ref,
    tail_inner_ref,
    tail_shared_ref,
    gain_ref,
    w_gate_inner_ref,
    w_shared_ref,
    w_step_ref,
    conv_inner_ref,
    conv_inner_bias_ref,
    conv_shared_ref,
    conv_shared_bias_ref,
    gated_gain_ref,
    w_out_ref,
    next_gain_ref,
    w_next_ref,
    new_ref,
    next_ref,
    kept_ref,
    kept_inner_ref,
    kept_shared_ref,
    gather_buf,
    small_out,
    small_buf,
    square_out,
    square_buf,
    part_out,
    part_buf,
    new_buf,
    stack,
    message,
    state_out,
    state_pool,
    state_lists,
    state_passing,
    state_final,
    state_second,
    news_pool,
    news_lists,
    news_passing,
    news_final,
    news_second,
    send_sem,
    recv_sem,
    route_send,
    route_recv,
):
    me = lax.axis_index("narrow")
    states = Route(
        0,
        table_ref,
        (state_pool, state_lists, state_passing, state_final, state_second),
        route_send,
        route_recv,
        side,
    )
    updates = Route(
        1,
        table_ref,
        (news_pool, news_lists, news_passing, news_final, news_second),
        route_send,
        route_recv,
        side,
    )
    block, tokens = hidden_ref.shape
    requests = start_ref.shape[0]
    length = tokens // requests
    width = block * count
    barrier = pltpu.get_barrier_semaphore()
    for step in range(1, count):
        pl.semaphore_signal(
            barrier, inc=1, device_id={"narrow": lax.rem(me + step, count)}, device_id_type=MESH
        )
    for half in (0, 1):
        for back in (0, 1):
            pl.semaphore_signal(
                barrier,
                inc=1,
                device_id={"wide": states.neighbour(half, back, 0)},
                device_id_type=MESH,
            )
    pl.semaphore_wait(barrier, count + 3)

    def send(source, target_buf, stage, step):
        pltpu.make_async_remote_copy(
            src_ref=source,
            dst_ref=target_buf.at[me],
            send_sem=send_sem.at[stage],
            recv_sem=recv_sem.at[stage],
            device_id={"narrow": lax.rem(me + step, count)},
            device_id_type=MESH,
        ).start()

    def finish(target_buf, stage):
        some = target_buf.at[pl.ds(0, count - 1)]
        both = pltpu.make_async_remote_copy(
            src_ref=some,
            dst_ref=some,
            send_sem=send_sem.at[stage],
            recv_sem=recv_sem.at[stage],
            device_id={"narrow": lax.rem(me + 1, count)},
            device_id_type=MESH,
        )
        both.wait_recv()
        both.wait_send()

    for step in range(1, count):
        send(hidden_ref, gather_buf, 0, step)
    gather_buf[me] = hidden_ref[...]
    half_rows = start_ref.shape[1] // 2
    states.fill(start_ref, half_rows)
    states.first(0)

    rows = lax.broadcasted_iota(jnp.int32, (tokens, tokens), 0)
    cols = lax.broadcasted_iota(jnp.int32, (tokens, tokens), 1)
    same = (rows >> 4) == (cols >> 4)
    tri = same & (cols <= rows)
    eye = rows == cols
    place = rows[:, :1] & (length - 1)
    acc = acc_ref[...]
    lane = lax.broadcasted_iota(jnp.int32, (tokens, block), 1)
    small_eye = lax.broadcasted_iota(jnp.int32, (block, block), 0) == lax.broadcasted_iota(
        jnp.int32, (block, block), 1
    )
    turn = small_eye.astype(BF16)

    def to_row(column):
        return jnp.sum(jnp.where(eye, column, 0.0), axis=0, keepdims=True)

    def gain_column(gains, n):
        return jnp.sum(
            jnp.where(small_eye, gains[:, n * block : (n + 1) * block], 0.0), axis=1, keepdims=True
        )

    def spread(values):
        return jnp.where(
            lane < 64, values[:, 0:1], jnp.where(lane < 128, values[:, 1:2], values[:, 2:3])
        )

    def scalars(ref, where, limit):
        return jnp.where(where < limit, ref[0], jnp.where(where < 2 * limit, ref[1], ref[2]))

    def normed(buf, gains):
        total = jnp.zeros((1, tokens), F32)
        for n in range(count):
            piece = buf[n].astype(F32)
            total = total + jnp.sum(piece * piece, axis=0, keepdims=True)
        factor = lax.rsqrt(total / width + EPSILON)
        for n in range(count):
            stack[n * block : (n + 1) * block, :] = (
                buf[n].astype(F32) * factor * gains[n]
            ).astype(BF16)

    gains_now = gain_ref[...].reshape(1, width)
    gains_now = [gain_column(gains_now, n) for n in range(count)]
    states.first(1)
    finish(gather_buf, 0)
    normed(gather_buf, gains_now)
    upright = (((0,), (0,)), ((), ()))
    small_out[...] = bdot(w_shared_ref[...], stack[...]).astype(BF16)
    for step in range(1, count):
        send(small_out, small_buf, 1, step)
    small_buf[me] = small_out[...]
    step_raw = bdot(w_step_ref[...], stack[...]).astype(BF16)
    both = lax.dot_general(
        w_gate_inner_ref[...], stack[...], upright, preferred_element_type=F32
    ).astype(BF16)
    gate = lax.dot_general(both[:block], turn, upright, preferred_element_type=F32)
    inner_bf = lax.dot_general(both[block:], turn, upright, preferred_element_type=F32).astype(BF16)
    states.first(2)

    def filtered(fresh, tail, weight, offset):
        total = offset + fresh * weight[3:4]
        for shift in (1, 2, 3):
            moved = jnp.where(
                place >= shift,
                pltpu.roll(fresh, shift, 0),
                pltpu.roll(tail, tokens - length + shift, 0),
            )
            total = total + moved * weight[3 - shift : 4 - shift]
        return jax.nn.silu(total)

    def padded(ref):
        total = jnp.zeros((tokens, ref.shape[2]), F32)
        at = lax.broadcasted_iota(jnp.int32, (tokens, requests), 0)
        slot = lax.broadcasted_iota(jnp.int32, (tokens, requests), 1)
        kept_rows = ref.shape[0]
        for q in range(kept_rows):
            put = ((at >> 4) == slot) & ((at & (length - 1)) == length - kept_rows + q)
            total = total + bdot(put.astype(BF16), ref[q])
        return total.astype(BF16)

    tail_inner = padded(tail_inner_ref)
    tail_shared = padded(tail_shared_ref)
    conv_i = filtered(
        inner_bf.astype(F32),
        tail_inner.astype(F32),
        conv_inner_ref[...].astype(F32),
        conv_inner_bias_ref[...],
    )

    heads = w_step_ref.shape[0]
    head_lane = lax.broadcasted_iota(jnp.int32, (heads, 128), 1)
    head_eye = (head_lane == lax.broadcasted_iota(jnp.int32, (heads, 128), 0)).astype(BF16)
    lane_row = lax.broadcasted_iota(jnp.int32, (1, 128), 1)
    raw = lax.dot_general(step_raw, head_eye, upright, preferred_element_type=F32) + scalars(
        bias_ref, lane_row, 1
    )
    steps = jnp.maximum(raw, 0.0) + jnp.log1p(jnp.exp(-jnp.abs(raw)))
    log_decay = steps * -jnp.exp(scalars(decay_ref, lane_row, 1))
    cumul = fdot(tri.astype(F32), log_decay)
    col_place = cols & (length - 1)
    ending = fdot((same & (col_place < acc)).astype(F32), log_decay)
    before = place < acc
    factor = jnp.where(before, jnp.exp(jnp.where(before, ending - cumul, 0.0)), 0.0) * steps
    decayed = jnp.exp(ending)
    weighted = (conv_i * spread(factor)).astype(BF16)

    states.first(3)
    finish(small_buf, 1)
    shared = lax.dot_general(
        small_buf[...].reshape(tokens, tokens),
        eye.astype(BF16),
        upright,
        preferred_element_type=F32,
    )
    conv_s = filtered(
        shared, tail_shared.astype(F32), conv_shared_ref[...].astype(F32), conv_shared_bias_ref[...]
    )
    b_part = conv_s[:, :128]
    c_part = conv_s[:, 128:]
    states.first(4)
    states.after(0)

    edge = rows[:, :1] & 15
    wanted = jnp.where(
        edge < 3, edge, jnp.where(edge < 6, edge - 3, jnp.where(edge < 9, edge - 6, edge - 9))
    )
    target = acc + wanted - 3
    sel_fresh = (same & (col_place == target)).astype(BF16)
    sel_tail = (same & (col_place == target + length)).astype(BF16)
    edge_i = bdot(sel_fresh, inner_bf) + bdot(sel_tail, tail_inner)
    edge_s = bdot(sel_fresh, shared.astype(BF16)) + bdot(sel_tail, tail_shared)
    pick_in = lax.broadcasted_iota(jnp.int32, (block, 128), 0)
    pick_out = lax.broadcasted_iota(jnp.int32, (block, 128), 1)
    last_head = (pick_in == pick_out + 128).astype(BF16)
    high = decayed.astype(BF16).astype(F32)
    low = decayed - high
    edges = jnp.where(
        edge < 3,
        edge_i[:, :128],
        jnp.where(
            edge < 6,
            bdot(edge_i.astype(BF16), last_head),
            jnp.where(
                edge < 9,
                edge_s[:, :128],
                jnp.where(
                    edge < 12, edge_s[:, 128:], jnp.where(edge == 12, high, jnp.where(edge == 13, low, 0.0))
                ),
            ),
        ),
    )
    message[:, 0:16, :] = weighted[:, :128].reshape(requests, length, 128)
    message[:, 16:32, :] = bdot(weighted, last_head).astype(BF16).reshape(requests, length, 128)
    message[:, 32:48, :] = b_part.astype(BF16).reshape(requests, length, 128)
    message[:, 48:64, :] = edges.astype(BF16).reshape(requests, length, 128)

    updates.fill(message, 32)
    updates.first(0)
    states.after(1)

    crossing = lax.dot_general(
        c_part, b_part, (((1,), (1,)), ((), ())), precision=HIGHEST, preferred_element_type=F32
    )
    direct = jnp.zeros((tokens, block), F32)
    for head in range(3):
        column = cumul[:, head : head + 1]
        gap = jnp.where(tri, column - to_row(column), 0.0)
        mixing = jnp.where(tri, jnp.exp(gap), 0.0) * to_row(steps[:, head : head + 1]) * crossing
        direct = direct + fdot(mixing, jnp.where((lane >> 6) == head, conv_i, 0.0))
    updates.first(1)
    carried = lax.dot_general(
        c_part.reshape(requests, length, 128),
        start_ref[...].astype(F32),
        (((2,), (2,)), ((0,), (0,))),
        precision=HIGHEST,
        preferred_element_type=F32,
    ).reshape(tokens, block)
    outputs = carried * spread(jnp.exp(cumul)) + direct + scalars(skip_ref, lane, 64) * conv_i
    gated = outputs * jax.nn.silu(gate)
    square_out[...] = lax.dot_general(
        jnp.ones((8, block), F32),
        gated * gated,
        (((1,), (1,)), ((), ())),
        precision=HIGHEST,
        preferred_element_type=F32,
    )
    for step in range(1, count):
        send(square_out, square_buf, 2, step)
    square_buf[me] = square_out[...]
    scaled = (gated * gated_gain_ref[...]).astype(BF16)
    scaled = lax.dot_general(
        turn, scaled, (((1,), (1,)), ((), ())), preferred_element_type=F32
    ).astype(BF16)
    part_out[...] = (
        lax.dot_general(w_out_ref[...], scaled, upright, preferred_element_type=F32)
        .astype(BF16)
        .reshape(count, block, tokens)
    )
    for step in range(1, count):
        send(part_out.at[lax.rem(me + step, count)], part_buf, 3, step)
    part_buf[me] = part_out[me]

    updates.first(2)
    states.after(2)
    updates.first(3)
    updates.first(4)
    updates.after(0)
    finish(square_buf, 2)
    squares = square_buf[0]
    for n in range(1, count):
        squares = squares + square_buf[n]
    factor_out = lax.rsqrt(squares[0:1] / width + EPSILON)
    finish(part_buf, 3)
    summed = part_buf[0].astype(F32)
    for n in range(1, count):
        summed = summed + part_buf[n].astype(F32)
    new_ref[...] = (hidden_ref[...].astype(F32) + summed * factor_out).astype(BF16)
    for step in range(1, count):
        send(new_ref, new_buf, 4, step)
    new_buf[me] = new_ref[...]
    updates.after(1)
    states.after(3)
    updates.after(2)
    updates.after(3)
    states.after(4)
    updates.after(4)
    states.collect(state_out, half_rows)
    updates.collect(message, 32)
    over = (((1,), (1,)), ((0,), (0,)))
    b_rows = message[:, 32:48, :]
    first = lax.dot_general(message[:, 0:16, :], b_rows, over, preferred_element_type=F32)
    last = lax.dot_general(message[:, 16:32, :], b_rows, over, preferred_element_type=F32)
    edges = message[:, 48:64, :].astype(F32)
    swap = ((rows >> 4) == (cols & 15)) & ((rows & 15) == (cols >> 4))
    by_row = bdot(swap.astype(BF16), message[:, 48:64, :].reshape(tokens, 128)).astype(BF16)
    for q in range(3):
        kept_inner_ref[q, :, 0:128] = by_row[16 * q : 16 * q + 16]
        kept_inner_ref[q, :, 128:192] = by_row[48 + 16 * q : 64 + 16 * q, 0:64]
        kept_shared_ref[q, :, 0:128] = by_row[96 + 16 * q : 112 + 16 * q]
        kept_shared_ref[q, :, 128:256] = by_row[144 + 16 * q : 160 + 16 * q]
    decay = edges[:, 12:13, :] + edges[:, 13:14, :]
    for head in range(3):
        low = 64 * head
        added = first[:, low : low + 64, :] if head < 2 else last[:, 0:64, :]
        kept_ref[:, low : low + 64, :] = (
            state_out[:, low : low + 64, :].astype(F32) * decay[:, :, head : head + 1] + added
        ).astype(BF16)
    finish(new_buf, 4)
    gains_next = next_gain_ref[...].reshape(1, width)
    normed(new_buf, [gain_column(gains_next, n) for n in range(count)])
    next_ref[...] = bdot(w_next_ref[...], stack[...]).astype(BF16)
    states.drain()
    updates.drain()


def hand_over_kernel(*refs):
    half = len(refs) // 2
    for source, target in zip(refs[:half], refs[half:]):
        target[...] = source[...]


def whole(memory_space=pltpu.VMEM):
    return pl.BlockSpec(memory_space=memory_space)


def local(
    count,
    hidden,
    start_state,
    tail_inner,
    tail_shared,
    input_gain,
    w_gate_inner,
    w_shared,
    w_step,
    step_bias,
    decay_log,
    conv_inner,
    conv_inner_bias,
    conv_shared,
    conv_shared_bias,
    skip_gain,
    gated_gain,
    w_output,
    next_gain,
    w_next,
    dealing,
    accepted,
    owners,
):
    tokens, block = hidden.shape
    requests, heads, head_size, states = start_state.shape
    start = start_state.reshape(requests, heads * head_size, states)
    routed = []
    for rows in (heads * head_size // 2, 32):
        routed += [
            pltpu.VMEM((2, 112, rows, 128), BF16),
            pltpu.VMEM((2, 2, 16, rows, 128), BF16),
            pltpu.VMEM((2, 2, 32, rows, 128), BF16),
            pltpu.VMEM((2, 32, rows, 128), BF16),
            pltpu.VMEM((2, 2, 48, rows, 128), BF16),
        ]
    shared_here = w_shared.shape[1]
    table, accepted_rows = pl.pallas_call(
        table_kernel,
        out_shape=(
            jax.ShapeDtypeStruct((8, 128), jnp.int32),
            jax.ShapeDtypeStruct((tokens, 1), jnp.int32),
        ),
        in_specs=[whole()] * 3,
        out_specs=(whole(), whole()),
        scratch_shapes=[pltpu.VMEM((dealing.shape[0], 8), F32)],
    )(dealing[None, :], owners[None, :], accepted[None, :])
    operands = (
        table,
        step_bias,
        decay_log,
        skip_gain,
        accepted_rows,
        hidden.T,
        start,
        tail_inner.transpose(1, 0, 2),
        tail_shared.transpose(1, 0, 2),
        input_gain,
        w_gate_inner,
        w_shared.T,
        w_step.T,
        conv_inner,
        conv_inner_bias[None, :],
        conv_shared,
        conv_shared_bias[None, :],
        gated_gain[None, :],
        w_output,
        next_gain,
        w_next.T,
    )
    blocks = pltpu.VMEM((count, block, tokens), BF16)
    results = pl.pallas_call(
        functools.partial(layer_kernel, count, SIDE),
        out_shape=(
            jax.ShapeDtypeStruct((block, tokens), BF16),
            jax.ShapeDtypeStruct((w_next.shape[1], tokens), BF16),
            jax.ShapeDtypeStruct(start.shape, BF16),
            jax.ShapeDtypeStruct((3, requests, tail_inner.shape[2]), BF16),
            jax.ShapeDtypeStruct((3, requests, tail_shared.shape[2]), BF16),
        ),
        in_specs=[whole(pltpu.SMEM)] * 4 + [whole()] * (len(operands) - 4),
        out_specs=(whole(),) * 5,
        scratch_shapes=[
            blocks,
            pltpu.VMEM((shared_here, tokens), BF16),
            pltpu.VMEM((count, shared_here, tokens), BF16),
            pltpu.VMEM((8, tokens), F32),
            pltpu.VMEM((count, 8, tokens), F32),
            blocks,
            blocks,
            blocks,
            pltpu.VMEM((count * block, tokens), BF16),
            pltpu.VMEM((requests, 64, 128), BF16),
            pltpu.VMEM(start.shape, BF16),
            *routed,
            pltpu.SemaphoreType.DMA((5,)),
            pltpu.SemaphoreType.DMA((5,)),
            pltpu.SemaphoreType.DMA((64,)),
            pltpu.SemaphoreType.DMA((64,)),
        ],
        compiler_params=pltpu.CompilerParams(
            collective_id=0, has_side_effects=True, vmem_limit_bytes=58 << 20
        ),
        cost_estimate=pl.CostEstimate(
            flops=4_000_000_000, bytes_accessed=100_000_000, transcendentals=0
        ),
    )(*operands)
    new_part, next_input, kept, kept_inner, kept_shared = pl.pallas_call(
        hand_over_kernel,
        out_shape=tuple(jax.ShapeDtypeStruct(one.shape, one.dtype) for one in results),
        in_specs=[whole()] * 5,
        out_specs=(whole(),) * 5,
    )(*results)
    return (
        new_part.T,
        next_input.T,
        kept.reshape(start_state.shape),
        kept_inner.transpose(1, 0, 2),
        kept_shared.transpose(1, 0, 2),
    )


def solution(mesh):
    placed = (
        P("wide", "narrow"),
        P("wide", "narrow", None, None),
        P("wide", None, "narrow"),
        P("wide", None, None),
        P(),
        P(None, "narrow"),
        P(None, "narrow"),
        P(None, "narrow"),
        P("narrow"),
        P("narrow"),
        P(None, "narrow"),
        P("narrow"),
        P(),
        P(),
        P("narrow"),
        P("narrow"),
        P("narrow", None),
        P(),
        P(None, "narrow"),
        P(),
        P(),
        P(),
    )
    return jax.shard_map(
        functools.partial(local, mesh.shape["narrow"]),
        mesh=mesh,
        in_specs=placed,
        out_specs=(
            P("wide", "narrow"),
            P("wide", "narrow"),
            P("wide", "narrow", None, None),
            P("wide", None, "narrow"),
            P("wide", None, None),
        ),
        check_vma=False,
    )
```

```python
import functools

import jax
import jax.numpy as jnp
from jax import lax
from jax.experimental import pallas as pl
from jax.experimental.pallas import tpu as pltpu
from jax.sharding import PartitionSpec as P

EPSILON = 1e-05
HIGHEST = lax.Precision.HIGHEST
MESH = pl.DeviceIdType.MESH
F32 = jnp.float32
BF16 = jnp.bfloat16


def fdot(a, b):
    return jnp.dot(a, b, precision=HIGHEST, preferred_element_type=F32)


def bdot(a, b):
    return jnp.dot(a, b, preferred_element_type=F32)


SIDE = 8
FAR = 4
BASE = (0, 0, 16, 32, 44)
STEPS = (4, 12, 16, 16)


def hop_base(dist):
    return jnp.where(dist <= 1, 0, jnp.where(dist == 2, 16, jnp.where(dist == 3, 32, 44)))


def table_values(dealing, owners, accepted, me, per=16):
    T = dealing.shape[1]
    ln = lax.broadcasted_iota(jnp.int32, (1, T), 1)
    sub = lax.broadcasted_iota(jnp.int32, (T, T), 0)
    pick = (sub == dealing).astype(BF16)
    row8 = lax.broadcasted_iota(jnp.int32, (8, T), 0)
    known = jnp.where(row8 == 0, owners, accepted).astype(F32).astype(BF16)
    per_slot = jnp.dot(known, pick, preferred_element_type=F32).astype(jnp.int32)
    owner = per_slot[0:1]
    acc = per_slot[1:2]
    sender = ln >> 4
    ys, zs = sender >> 3, sender & 7
    yo, zo = owner >> 3, owner & 7
    me_y, me_z = me // SIDE, lax.rem(me, SIDE)
    halves = []
    keys, starts = [], []
    for fs, fo, gs, go in ((zs, zo, ys, yo), (ys, yo, zs, zo)):
        d1 = (fo - fs) & 7
        back1 = jnp.where((d1 > FAR) | ((d1 == FAR) & ((go & 1) == 1)), 1, 0)
        dist1 = jnp.where(back1 == 1, SIDE - d1, d1)
        d2 = (go - gs) & 7
        back2 = jnp.where((d2 > FAR) | ((d2 == FAR) & ((fs & 1) == 1)), 1, 0)
        dist2 = jnp.where(back2 == 1, SIDE - d2, d2)
        for group, back, dist in ((sender, back1, dist1), (owner, back2, dist2)):
            level = FAR + jnp.where(back == 1, dist, -dist)
            starts.append((16 * group, back))
            keys.append(((group * 16 + level) * T + ln).astype(F32))
        halves.append((back1, dist1, back2, dist2))
    starts.append((16 * owner, 0))
    keys.append((owner * T + dealing).astype(F32))
    stacked = jnp.where(row8 == 0, keys[0], jnp.where(row8 == 1, keys[1], jnp.where(row8 == 2, keys[2], jnp.where(row8 == 3, keys[3], keys[4]))))
    return ln, sender, owner, acc, me_y, me_z, halves, keys, starts, stacked


def places_of(found, starts):
    ranks = [count.astype(jnp.int32) - start for count, (start, _) in zip(found, starts)]
    return [jnp.where(back == 1, 15 - rank, rank) for rank, (_, back) in zip(ranks, starts)]


def finish_tables(ln, sender, owner, acc, me, halves, places):
    T = ln.shape[1]
    lane = lax.broadcasted_iota(jnp.int32, (128, 128), 1)
    sub = lax.broadcasted_iota(jnp.int32, (128, 128), 0)
    t = lax.broadcasted_iota(jnp.int32, (128, 1), 0)
    def to_row(column):
        return jnp.sum(jnp.where(lane == sub, column.astype(F32), 0.0), axis=0, keepdims=True).astype(jnp.int32)
    def lookup(want, key, value, missing):
        return to_row(jnp.max(jnp.where(want == key, value, missing).astype(F32), axis=1, keepdims=True))
    me_y, me_z = me // SIDE, lax.rem(me, SIDE)
    out = []
    for h in (0, 1):
        back1, dist1, back2, dist2 = halves[h]
        pos1, pos2 = places[2 * h], places[2 * h + 1]
        loc = jnp.where(
            dist1 == 0, ln & 15, jnp.minimum(16 + back1 * 48 + hop_base(dist1) + pos1, 111)
        )
        out.append(lookup(me * 32 + t, sender * 32 + back1 * 16 + pos1, ln & 15, 0))
        back_t = jnp.where(t >= 48, 1, 0)
        q = t - 48 * back_t
        hop = jnp.where(q < 4, 4, jnp.where(q < 16, 3, jnp.where(q < 32, 2, 1)))
        i = q - jnp.where(q < 4, 0, jnp.where(q < 16, 4, jnp.where(q < 32, 16, 32)))
        move = jnp.where(back_t == 1, -hop, hop)
        if h == 0:
            dest = ((me_y + move) & 7) * SIDE + me_z
        else:
            dest = me_y * SIDE + ((me_z + move) & 7)
        out.append(lookup(((dest * 2 + back_t) * 8 + hop) * 16 + i, ((owner * 2 + back2) * 8 + dist2) * 16 + pos2, loc, -1))
        out.append(lookup(me * 16 + t, owner * 16 + places[4], jnp.where(dist2 == 0, loc, 128 + jnp.minimum(back2 * 16 + pos2, 31)), 0))
    out.append(lookup(me * 16 + t, ln, acc, 0))
    out.append(out[-1])
    r = lax.broadcasted_iota(jnp.int32, (8, 128), 0)
    table = jnp.zeros((8, 128), jnp.int32)
    for k in range(7):
        table = jnp.where(r == k, out[k], table)
    return table


def table_kernel(dealing_ref, owners_ref, accepted_ref, table_ref, count_ref, columns):
    me = lax.axis_index("wide")
    ln, sender, owner, acc, me_y, me_z, halves, keys, starts, stacked = table_values(
        dealing_ref[...], owners_ref[...], accepted_ref[...], me
    )
    columns[...] = jnp.transpose(stacked)
    total = ln.shape[1]
    chunk = 64

    def count(step, found):
        part = columns[pl.ds(pl.multiple_of(step * chunk, chunk), chunk), :]
        return tuple(
            found[k]
            + jnp.sum(
                jnp.where(part[:, k : k + 1] < keys[k], 1.0, 0.0),
                axis=0,
                keepdims=True,
            )
            for k in range(5)
        )

    found = lax.fori_loop(
        0, total // chunk, count, tuple(jnp.zeros((1, total), F32) for _ in range(5))
    )
    table_ref[...] = finish_tables(
        ln, sender, owner, acc, me, halves, places_of(found, starts)
    )
    tokens = count_ref.shape[0]
    slot = lax.broadcasted_iota(jnp.int32, (tokens, total), 0) >> 4
    at = lax.broadcasted_iota(jnp.int32, (tokens, total), 1)
    count_ref[...] = jnp.sum(
        jnp.where(at == me * 16 + slot, acc, 0).astype(F32), axis=1, keepdims=True
    ).astype(jnp.int32)


CAPS = (16, 16, 12, 4)
OFFS = (0, 16, 32, 44)
SECOND_OFFS = (0, 4, 16, 32)


class Route:
    def __init__(self, number, table, refs, send_sem, recv_sem, side):
        self.number, self.table = number, table
        self.send_sem, self.recv_sem, self.side = send_sem, recv_sem, side
        self.pool, self.lists, self.passing, self.final, self.second = refs

    def neighbour(self, half, back, phase):
        me = lax.axis_index("wide")
        side = self.side
        y, z = me // side, lax.rem(me, side)
        move = side - 1 if back else 1
        if (half == 0) == (phase == 0):
            return y * side + lax.rem(z + move, side)
        return lax.rem(y + move, side) * side + z

    def copy(self, phase, half, back, hop):
        if phase == 0:
            low = 16 + 48 * back
            if hop == 0:
                source = self.lists.at[half, back]
            else:
                source = self.pool.at[half, pl.ds(low + OFFS[hop - 1], CAPS[hop])]
            target = self.pool.at[half, pl.ds(low + OFFS[hop], CAPS[hop])]
        else:
            size = CAPS[3 - hop]
            source = self.second.at[half, back, pl.ds(SECOND_OFFS[hop], size)]
            if hop < 3:
                target = self.passing.at[half, back, pl.ds(SECOND_OFFS[hop], size)]
            else:
                target = self.final.at[half, pl.ds(16 * back, size)]
        at = (((self.number * 2 + phase) * 2 + half) * 2 + back) * 4 + hop
        return pltpu.make_async_remote_copy(
            src_ref=source,
            dst_ref=target,
            send_sem=self.send_sem.at[at],
            recv_sem=self.recv_sem.at[at],
            device_id={"wide": self.neighbour(half, back, phase)},
            device_id_type=MESH,
        )

    def each(self, phase, hop):
        return [self.copy(phase, half, back, hop) for half in (0, 1) for back in (0, 1)]

    def fill(self, blocks, rows):
        for half in (0, 1):
            low = half * rows

            def own(i, carry):
                self.pool[half, i] = blocks[i, low : low + rows, :]
                return carry

            lax.fori_loop(0, 16, own, 0)
            for back in (0, 1):

                def listed(i, carry):
                    self.lists[half, back, i] = blocks[jnp.clip(self.table[3 * half, 16 * back + i], 0, 15), low : low + rows, :]
                    return carry

                lax.fori_loop(0, 16, listed, 0)

    def first(self, hop):
        if hop > 0:
            for copy in self.each(0, hop - 1):
                copy.wait_recv()
        if hop < 4:
            for copy in self.each(0, hop):
                copy.start()

    def after(self, hop):
        if hop > 0:
            for copy in self.each(1, hop - 1):
                copy.wait_recv()
        if hop == 4:
            return
        low = SECOND_OFFS[hop]
        size = CAPS[3 - hop]
        known = CAPS[4 - hop] if hop > 0 else 0
        for half in (0, 1):
            for back in (0, 1):

                def merged(i, carry):
                    at = self.table[3 * half + 1, 48 * back + low + i]
                    mine = self.pool[half, jnp.clip(at, 0, 111)]
                    came = self.passing[half, back, SECOND_OFFS[hop - 1] + i]
                    self.second[half, back, low + i] = jnp.where(at >= 0, mine, came)
                    return carry

                def fresh(i, carry):
                    at = self.table[3 * half + 1, 48 * back + low + i]
                    self.second[half, back, low + i] = self.pool[half, jnp.clip(at, 0, 111)]
                    return carry

                if known:
                    lax.fori_loop(0, known, merged, 0)
                if known < size:
                    lax.fori_loop(known, size, fresh, 0)
        for copy in self.each(1, hop):
            copy.start()

    def collect(self, blocks, rows):
        for half in (0, 1):
            low = half * rows

            def take(k, carry):
                at = self.table[3 * half + 2, k]
                here = self.pool[half, jnp.clip(jnp.where(at < 128, at, 0), 0, 111)]
                came = self.final[half, jnp.clip(at - 128, 0, 31)]
                blocks[k, low : low + rows, :] = jnp.where(at < 128, here, came)
                return carry

            lax.fori_loop(0, 16, take, 0)

    def drain(self):
        for phase in (0, 1):
            for hop in range(4):
                for copy in self.each(phase, hop):
                    copy.wait_send()


def layer_kernel(
    count,
    side,
    table_ref,
    bias_ref,
    decay_ref,
    skip_ref,
    acc_ref,
    hidden_ref,
    start_ref,
    tail_inner_ref,
    tail_shared_ref,
    gain_ref,
    w_gate_inner_ref,
    w_shared_ref,
    w_step_ref,
    conv_inner_ref,
    conv_inner_bias_ref,
    conv_shared_ref,
    conv_shared_bias_ref,
    gated_gain_ref,
    w_out_ref,
    next_gain_ref,
    w_next_ref,
    new_ref,
    next_ref,
    kept_ref,
    kept_inner_ref,
    kept_shared_ref,
    gather_buf,
    small_out,
    small_buf,
    square_out,
    square_buf,
    part_out,
    part_buf,
    new_buf,
    stack,
    message,
    state_out,
    state_pool,
    state_lists,
    state_passing,
    state_final,
    state_second,
    news_pool,
    news_lists,
    news_passing,
    news_final,
    news_second,
    send_sem,
    recv_sem,
    route_send,
    route_recv,
):
    me = lax.axis_index("narrow")
    states = Route(
        0,
        table_ref,
        (state_pool, state_lists, state_passing, state_final, state_second),
        route_send,
        route_recv,
        side,
    )
    updates = Route(
        1,
        table_ref,
        (news_pool, news_lists, news_passing, news_final, news_second),
        route_send,
        route_recv,
        side,
    )
    block, tokens = hidden_ref.shape
    requests = start_ref.shape[0]
    length = tokens // requests
    width = block * count
    barrier = pltpu.get_barrier_semaphore()
    for step in range(1, count):
        pl.semaphore_signal(
            barrier, inc=1, device_id={"narrow": lax.rem(me + step, count)}, device_id_type=MESH
        )
    for half in (0, 1):
        for back in (0, 1):
            pl.semaphore_signal(
                barrier,
                inc=1,
                device_id={"wide": states.neighbour(half, back, 0)},
                device_id_type=MESH,
            )
    pl.semaphore_wait(barrier, count + 3)

    def send(source, target_buf, stage, step):
        pltpu.make_async_remote_copy(
            src_ref=source,
            dst_ref=target_buf.at[me],
            send_sem=send_sem.at[stage],
            recv_sem=recv_sem.at[stage],
            device_id={"narrow": lax.rem(me + step, count)},
            device_id_type=MESH,
        ).start()

    def finish(target_buf, stage):
        some = target_buf.at[pl.ds(0, count - 1)]
        both = pltpu.make_async_remote_copy(
            src_ref=some,
            dst_ref=some,
            send_sem=send_sem.at[stage],
            recv_sem=recv_sem.at[stage],
            device_id={"narrow": lax.rem(me + 1, count)},
            device_id_type=MESH,
        )
        both.wait_recv()
        both.wait_send()

    for step in range(1, count):
        send(hidden_ref, gather_buf, 0, step)
    gather_buf[me] = hidden_ref[...]
    half_rows = start_ref.shape[1] // 2
    states.fill(start_ref, half_rows)
    states.first(0)

    rows = lax.broadcasted_iota(jnp.int32, (tokens, tokens), 0)
    cols = lax.broadcasted_iota(jnp.int32, (tokens, tokens), 1)
    same = (rows >> 4) == (cols >> 4)
    tri = same & (cols <= rows)
    eye = rows == cols
    place = rows[:, :1] & (length - 1)
    acc = acc_ref[...]
    lane = lax.broadcasted_iota(jnp.int32, (tokens, block), 1)
    small_eye = lax.broadcasted_iota(jnp.int32, (block, block), 0) == lax.broadcasted_iota(
        jnp.int32, (block, block), 1
    )
    turn = small_eye.astype(BF16)

    def to_row(column):
        return jnp.sum(jnp.where(eye, column, 0.0), axis=0, keepdims=True)

    def gain_column(gains, n):
        return jnp.sum(
            jnp.where(small_eye, gains[:, n * block : (n + 1) * block], 0.0), axis=1, keepdims=True
        )

    def spread(values):
        return jnp.where(
            lane < 64, values[:, 0:1], jnp.where(lane < 128, values[:, 1:2], values[:, 2:3])
        )

    def scalars(ref, where, limit):
        return jnp.where(where < limit, ref[0], jnp.where(where < 2 * limit, ref[1], ref[2]))

    def normed(buf, gains):
        total = jnp.zeros((1, tokens), F32)
        for n in range(count):
            piece = buf[n].astype(F32)
            total = total + jnp.sum(piece * piece, axis=0, keepdims=True)
        factor = lax.rsqrt(total / width + EPSILON)
        for n in range(count):
            stack[n * block : (n + 1) * block, :] = (
                buf[n].astype(F32) * factor * gains[n]
            ).astype(BF16)

    gains_now = gain_ref[...].reshape(1, width)
    gains_now = [gain_column(gains_now, n) for n in range(count)]
    states.first(1)
    finish(gather_buf, 0)
    normed(gather_buf, gains_now)
    upright = (((0,), (0,)), ((), ()))
    small_out[...] = bdot(w_shared_ref[...], stack[...]).astype(BF16)
    for step in range(1, count):
        send(small_out, small_buf, 1, step)
    small_buf[me] = small_out[...]
    step_raw = bdot(w_step_ref[...], stack[...]).astype(BF16)
    both = lax.dot_general(
        w_gate_inner_ref[...], stack[...], upright, preferred_element_type=F32
    ).astype(BF16)
    gate = lax.dot_general(both[:block], turn, upright, preferred_element_type=F32)
    inner_bf = lax.dot_general(both[block:], turn, upright, preferred_element_type=F32).astype(BF16)
    states.first(2)

    def filtered(fresh, tail, weight, offset):
        total = offset + fresh * weight[3:4]
        for shift in (1, 2, 3):
            moved = jnp.where(
                place >= shift,
                pltpu.roll(fresh, shift, 0),
                pltpu.roll(tail, tokens - length + shift, 0),
            )
            total = total + moved * weight[3 - shift : 4 - shift]
        return jax.nn.silu(total)

    def padded(ref):
        total = jnp.zeros((tokens, ref.shape[2]), F32)
        at = lax.broadcasted_iota(jnp.int32, (tokens, requests), 0)
        slot = lax.broadcasted_iota(jnp.int32, (tokens, requests), 1)
        kept_rows = ref.shape[0]
        for q in range(kept_rows):
            put = ((at >> 4) == slot) & ((at & (length - 1)) == length - kept_rows + q)
            total = total + bdot(put.astype(BF16), ref[q])
        return total.astype(BF16)

    tail_inner = padded(tail_inner_ref)
    tail_shared = padded(tail_shared_ref)
    conv_i = filtered(
        inner_bf.astype(F32),
        tail_inner.astype(F32),
        conv_inner_ref[...].astype(F32),
        conv_inner_bias_ref[...],
    )

    heads = w_step_ref.shape[0]
    head_lane = lax.broadcasted_iota(jnp.int32, (heads, 128), 1)
    head_eye = (head_lane == lax.broadcasted_iota(jnp.int32, (heads, 128), 0)).astype(BF16)
    lane_row = lax.broadcasted_iota(jnp.int32, (1, 128), 1)
    raw = lax.dot_general(step_raw, head_eye, upright, preferred_element_type=F32) + scalars(
        bias_ref, lane_row, 1
    )
    steps = jnp.maximum(raw, 0.0) + jnp.log1p(jnp.exp(-jnp.abs(raw)))
    log_decay = steps * -jnp.exp(scalars(decay_ref, lane_row, 1))
    cumul = fdot(tri.astype(F32), log_decay)
    col_place = cols & (length - 1)
    ending = fdot((same & (col_place < acc)).astype(F32), log_decay)
    before = place < acc
    factor = jnp.where(before, jnp.exp(jnp.where(before, ending - cumul, 0.0)), 0.0) * steps
    decayed = jnp.exp(ending)
    weighted = (conv_i * spread(factor)).astype(BF16)

    states.first(3)
    finish(small_buf, 1)
    shared = lax.dot_general(
        small_buf[...].reshape(tokens, tokens),
        eye.astype(BF16),
        upright,
        preferred_element_type=F32,
    )
    conv_s = filtered(
        shared, tail_shared.astype(F32), conv_shared_ref[...].astype(F32), conv_shared_bias_ref[...]
    )
    b_part = conv_s[:, :128]
    c_part = conv_s[:, 128:]
    states.first(4)
    states.after(0)

    edge = rows[:, :1] & 15
    wanted = jnp.where(
        edge < 3, edge, jnp.where(edge < 6, edge - 3, jnp.where(edge < 9, edge - 6, edge - 9))
    )
    target = acc + wanted - 3
    sel_fresh = (same & (col_place == target)).astype(BF16)
    sel_tail = (same & (col_place == target + length)).astype(BF16)
    edge_i = bdot(sel_fresh, inner_bf) + bdot(sel_tail, tail_inner)
    edge_s = bdot(sel_fresh, shared.astype(BF16)) + bdot(sel_tail, tail_shared)
    pick_in = lax.broadcasted_iota(jnp.int32, (block, 128), 0)
    pick_out = lax.broadcasted_iota(jnp.int32, (block, 128), 1)
    last_head = (pick_in == pick_out + 128).astype(BF16)
    high = decayed.astype(BF16).astype(F32)
    low = decayed - high
    edges = jnp.where(
        edge < 3,
        edge_i[:, :128],
        jnp.where(
            edge < 6,
            bdot(edge_i.astype(BF16), last_head),
            jnp.where(
                edge < 9,
                edge_s[:, :128],
                jnp.where(
                    edge < 12, edge_s[:, 128:], jnp.where(edge == 12, high, jnp.where(edge == 13, low, 0.0))
                ),
            ),
        ),
    )
    message[:, 0:16, :] = weighted[:, :128].reshape(requests, length, 128)
    message[:, 16:32, :] = bdot(weighted, last_head).astype(BF16).reshape(requests, length, 128)
    message[:, 32:48, :] = b_part.astype(BF16).reshape(requests, length, 128)
    message[:, 48:64, :] = edges.astype(BF16).reshape(requests, length, 128)

    updates.fill(message, 32)
    updates.first(0)
    states.after(1)

    crossing = lax.dot_general(
        c_part, b_part, (((1,), (1,)), ((), ())), precision=HIGHEST, preferred_element_type=F32
    )
    direct = jnp.zeros((tokens, block), F32)
    for head in range(3):
        column = cumul[:, head : head + 1]
        gap = jnp.where(tri, column - to_row(column), 0.0)
        mixing = jnp.where(tri, jnp.exp(gap), 0.0) * to_row(steps[:, head : head + 1]) * crossing
        direct = direct + fdot(mixing, jnp.where((lane >> 6) == head, conv_i, 0.0))
    updates.first(1)
    carried = lax.dot_general(
        c_part.reshape(requests, length, 128),
        start_ref[...].astype(F32),
        (((2,), (2,)), ((0,), (0,))),
        precision=HIGHEST,
        preferred_element_type=F32,
    ).reshape(tokens, block)
    outputs = carried * spread(jnp.exp(cumul)) + direct + scalars(skip_ref, lane, 64) * conv_i
    gated = outputs * jax.nn.silu(gate)
    square_out[...] = lax.dot_general(
        jnp.ones((8, block), F32),
        gated * gated,
        (((1,), (1,)), ((), ())),
        precision=HIGHEST,
        preferred_element_type=F32,
    )
    for step in range(1, count):
        send(square_out, square_buf, 2, step)
    square_buf[me] = square_out[...]
    scaled = (gated * gated_gain_ref[...]).astype(BF16)
    scaled = lax.dot_general(
        turn, scaled, (((1,), (1,)), ((), ())), preferred_element_type=F32
    ).astype(BF16)
    part_out[...] = (
        lax.dot_general(w_out_ref[...], scaled, upright, preferred_element_type=F32)
        .astype(BF16)
        .reshape(count, block, tokens)
    )
    for step in range(1, count):
        send(part_out.at[lax.rem(me + step, count)], part_buf, 3, step)
    part_buf[me] = part_out[me]

    updates.first(2)
    states.after(2)
    updates.first(3)
    updates.first(4)
    updates.after(0)
    finish(square_buf, 2)
    squares = square_buf[0]
    for n in range(1, count):
        squares = squares + square_buf[n]
    factor_out = lax.rsqrt(squares[0:1] / width + EPSILON)
    finish(part_buf, 3)
    summed = part_buf[0].astype(F32)
    for n in range(1, count):
        summed = summed + part_buf[n].astype(F32)
    new_ref[...] = (hidden_ref[...].astype(F32) + summed * factor_out).astype(BF16)
    for step in range(1, count):
        send(new_ref, new_buf, 4, step)
    new_buf[me] = new_ref[...]
    updates.after(1)
    states.after(3)
    updates.after(2)
    updates.after(3)
    states.after(4)
    updates.after(4)
    states.collect(state_out, half_rows)
    updates.collect(message, 32)
    over = (((1,), (1,)), ((0,), (0,)))
    b_rows = message[:, 32:48, :]
    first = lax.dot_general(message[:, 0:16, :], b_rows, over, preferred_element_type=F32)
    last = lax.dot_general(message[:, 16:32, :], b_rows, over, preferred_element_type=F32)
    edges = message[:, 48:64, :].astype(F32)
    swap = ((rows >> 4) == (cols & 15)) & ((rows & 15) == (cols >> 4))
    by_row = bdot(swap.astype(BF16), message[:, 48:64, :].reshape(tokens, 128)).astype(BF16)
    for q in range(3):
        kept_inner_ref[q, :, 0:128] = by_row[16 * q : 16 * q + 16]
        kept_inner_ref[q, :, 128:192] = by_row[48 + 16 * q : 64 + 16 * q, 0:64]
        kept_shared_ref[q, :, 0:128] = by_row[96 + 16 * q : 112 + 16 * q]
        kept_shared_ref[q, :, 128:256] = by_row[144 + 16 * q : 160 + 16 * q]
    decay = edges[:, 12:13, :] + edges[:, 13:14, :]
    for head in range(3):
        low = 64 * head
        added = first[:, low : low + 64, :] if head < 2 else last[:, 0:64, :]
        kept_ref[:, low : low + 64, :] = (
            state_out[:, low : low + 64, :].astype(F32) * decay[:, :, head : head + 1] + added
        ).astype(BF16)
    finish(new_buf, 4)
    gains_next = next_gain_ref[...].reshape(1, width)
    normed(new_buf, [gain_column(gains_next, n) for n in range(count)])
    next_ref[...] = bdot(w_next_ref[...], stack[...]).astype(BF16)
    states.drain()
    updates.drain()


def hand_over_kernel(*refs):
    half = len(refs) // 2
    for source, target in zip(refs[:half], refs[half:]):
        target[...] = source[...]


def whole(memory_space=pltpu.VMEM):
    return pl.BlockSpec(memory_space=memory_space)


def local(
    count,
    hidden,
    start_state,
    tail_inner,
    tail_shared,
    input_gain,
    w_gate_inner,
    w_shared,
    w_step,
    step_bias,
    decay_log,
    conv_inner,
    conv_inner_bias,
    conv_shared,
    conv_shared_bias,
    skip_gain,
    gated_gain,
    w_output,
    next_gain,
    w_next,
    dealing,
    accepted,
    owners,
):
    tokens, block = hidden.shape
    requests, heads, head_size, states = start_state.shape
    start = start_state.reshape(requests, heads * head_size, states)
    routed = []
    for rows in (heads * head_size // 2, 32):
        routed += [
            pltpu.VMEM((2, 112, rows, 128), BF16),
            pltpu.VMEM((2, 2, 16, rows, 128), BF16),
            pltpu.VMEM((2, 2, 32, rows, 128), BF16),
            pltpu.VMEM((2, 32, rows, 128), BF16),
            pltpu.VMEM((2, 2, 48, rows, 128), BF16),
        ]
    shared_here = w_shared.shape[1]
    table, accepted_rows = pl.pallas_call(
        table_kernel,
        out_shape=(
            jax.ShapeDtypeStruct((8, 128), jnp.int32),
            jax.ShapeDtypeStruct((tokens, 1), jnp.int32),
        ),
        in_specs=[whole()] * 3,
        out_specs=(whole(), whole()),
        scratch_shapes=[pltpu.VMEM((dealing.shape[0], 8), F32)],
    )(dealing[None, :], owners[None, :], accepted[None, :])
    operands = (
        table,
        step_bias,
        decay_log,
        skip_gain,
        accepted_rows,
        hidden.T,
        start,
        tail_inner.transpose(1, 0, 2),
        tail_shared.transpose(1, 0, 2),
        input_gain,
        w_gate_inner,
        w_shared.T,
        w_step.T,
        conv_inner,
        conv_inner_bias[None, :],
        conv_shared,
        conv_shared_bias[None, :],
        gated_gain[None, :],
        w_output,
        next_gain,
        w_next.T,
    )
    blocks = pltpu.VMEM((count, block, tokens), BF16)
    results = pl.pallas_call(
        functools.partial(layer_kernel, count, SIDE),
        out_shape=(
            jax.ShapeDtypeStruct((block, tokens), BF16),
            jax.ShapeDtypeStruct((w_next.shape[1], tokens), BF16),
            jax.ShapeDtypeStruct(start.shape, BF16),
            jax.ShapeDtypeStruct((3, requests, tail_inner.shape[2]), BF16),
            jax.ShapeDtypeStruct((3, requests, tail_shared.shape[2]), BF16),
        ),
        in_specs=[whole(pltpu.SMEM)] * 4 + [whole()] * (len(operands) - 4),
        out_specs=(whole(),) * 5,
        scratch_shapes=[
            blocks,
            pltpu.VMEM((shared_here, tokens), BF16),
            pltpu.VMEM((count, shared_here, tokens), BF16),
            pltpu.VMEM((8, tokens), F32),
            pltpu.VMEM((count, 8, tokens), F32),
            blocks,
            blocks,
            blocks,
            pltpu.VMEM((count * block, tokens), BF16),
            pltpu.VMEM((requests, 64, 128), BF16),
            pltpu.VMEM(start.shape, BF16),
            *routed,
            pltpu.SemaphoreType.DMA((5,)),
            pltpu.SemaphoreType.DMA((5,)),
            pltpu.SemaphoreType.DMA((64,)),
            pltpu.SemaphoreType.DMA((64,)),
        ],
        compiler_params=pltpu.CompilerParams(
            collective_id=0, has_side_effects=True, vmem_limit_bytes=58 << 20
        ),
        cost_estimate=pl.CostEstimate(
            flops=4_000_000_000, bytes_accessed=100_000_000, transcendentals=0
        ),
    )(*operands)
    new_part, next_input, kept, kept_inner, kept_shared = pl.pallas_call(
        hand_over_kernel,
        out_shape=tuple(jax.ShapeDtypeStruct(one.shape, one.dtype) for one in results),
        in_specs=[whole()] * 5,
        out_specs=(whole(),) * 5,
    )(*results)
    return (
        new_part.T,
        next_input.T,
        kept.reshape(start_state.shape),
        kept_inner.transpose(1, 0, 2),
        kept_shared.transpose(1, 0, 2),
    )


def solution(mesh):
    placed = (
        P("wide", "narrow"),
        P("wide", "narrow", None, None),
        P("wide", None, "narrow"),
        P("wide", None, None),
        P(),
        P(None, "narrow"),
        P(None, "narrow"),
        P(None, "narrow"),
        P("narrow"),
        P("narrow"),
        P(None, "narrow"),
        P("narrow"),
        P(),
        P(),
        P("narrow"),
        P("narrow"),
        P("narrow", None),
        P(),
        P(None, "narrow"),
        P(),
        P(),
        P(),
    )
    return jax.shard_map(
        functools.partial(local, mesh.shape["narrow"]),
        mesh=mesh,
        in_specs=placed,
        out_specs=(
            P("wide", "narrow"),
            P("wide", "narrow"),
            P("wide", "narrow", None, None),
            P("wide", None, "narrow"),
            P("wide", None, None),
        ),
        check_vma=False,
    )
```

```python
import functools

import jax
import jax.numpy as jnp
from jax import lax
from jax.experimental import pallas as pl
from jax.experimental.pallas import tpu as pltpu
from jax.sharding import PartitionSpec as P

EPSILON = 1e-05
HIGHEST = lax.Precision.HIGHEST
MESH = pl.DeviceIdType.MESH
F32 = jnp.float32
BF16 = jnp.bfloat16


def fdot(a, b):
    return jnp.dot(a, b, precision=HIGHEST, preferred_element_type=F32)


def bdot(a, b):
    return jnp.dot(a, b, preferred_element_type=F32)


SIDE = 8
FAR = 4
BASE = (0, 0, 16, 32, 44)
STEPS = (4, 12, 16, 16)


def hop_base(dist):
    return jnp.where(dist <= 1, 0, jnp.where(dist == 2, 16, jnp.where(dist == 3, 32, 44)))


def table_values(dealing, owners, accepted, me, per=16):
    T = dealing.shape[1]
    ln = lax.broadcasted_iota(jnp.int32, (1, T), 1)
    sub = lax.broadcasted_iota(jnp.int32, (T, T), 0)
    pick = (sub == dealing).astype(BF16)
    row8 = lax.broadcasted_iota(jnp.int32, (8, T), 0)
    known = jnp.where(row8 == 0, owners, accepted).astype(F32).astype(BF16)
    per_slot = jnp.dot(known, pick, preferred_element_type=F32).astype(jnp.int32)
    owner = per_slot[0:1]
    acc = per_slot[1:2]
    sender = ln >> 4
    ys, zs = sender >> 3, sender & 7
    yo, zo = owner >> 3, owner & 7
    me_y, me_z = me // SIDE, lax.rem(me, SIDE)
    halves = []
    keys, starts = [], []
    for fs, fo, gs, go in ((zs, zo, ys, yo), (ys, yo, zs, zo)):
        d1 = (fo - fs) & 7
        back1 = jnp.where((d1 > FAR) | ((d1 == FAR) & ((go & 1) == 1)), 1, 0)
        dist1 = jnp.where(back1 == 1, SIDE - d1, d1)
        d2 = (go - gs) & 7
        back2 = jnp.where((d2 > FAR) | ((d2 == FAR) & ((fs & 1) == 1)), 1, 0)
        dist2 = jnp.where(back2 == 1, SIDE - d2, d2)
        for group, back, dist in ((sender, back1, dist1), (owner, back2, dist2)):
            level = FAR + jnp.where(back == 1, dist, -dist)
            starts.append((16 * group, back))
            keys.append(((group * 16 + level) * T + ln).astype(F32))
        halves.append((back1, dist1, back2, dist2))
    starts.append((16 * owner, 0))
    keys.append((owner * T + dealing).astype(F32))
    stacked = jnp.where(row8 == 0, keys[0], jnp.where(row8 == 1, keys[1], jnp.where(row8 == 2, keys[2], jnp.where(row8 == 3, keys[3], keys[4]))))
    return ln, sender, owner, acc, me_y, me_z, halves, keys, starts, stacked


def places_of(found, starts):
    ranks = [count.astype(jnp.int32) - start for count, (start, _) in zip(found, starts)]
    return [jnp.where(back == 1, 15 - rank, rank) for rank, (_, back) in zip(ranks, starts)]


def finish_tables(ln, sender, owner, acc, me, halves, places):
    T = ln.shape[1]
    lane = lax.broadcasted_iota(jnp.int32, (128, 128), 1)
    sub = lax.broadcasted_iota(jnp.int32, (128, 128), 0)
    t = lax.broadcasted_iota(jnp.int32, (128, 1), 0)
    def to_row(column):
        return jnp.sum(jnp.where(lane == sub, column.astype(F32), 0.0), axis=0, keepdims=True).astype(jnp.int32)
    def lookup(want, key, value, missing):
        return to_row(jnp.max(jnp.where(want == key, value, missing).astype(F32), axis=1, keepdims=True))
    me_y, me_z = me // SIDE, lax.rem(me, SIDE)
    out = []
    for h in (0, 1):
        back1, dist1, back2, dist2 = halves[h]
        pos1, pos2 = places[2 * h], places[2 * h + 1]
        loc = jnp.where(
            dist1 == 0, ln & 15, jnp.minimum(16 + back1 * 48 + hop_base(dist1) + pos1, 111)
        )
        out.append(lookup(me * 32 + t, sender * 32 + back1 * 16 + pos1, ln & 15, 0))
        back_t = jnp.where(t >= 48, 1, 0)
        q = t - 48 * back_t
        hop = jnp.where(q < 4, 4, jnp.where(q < 16, 3, jnp.where(q < 32, 2, 1)))
        i = q - jnp.where(q < 4, 0, jnp.where(q < 16, 4, jnp.where(q < 32, 16, 32)))
        move = jnp.where(back_t == 1, -hop, hop)
        if h == 0:
            dest = ((me_y + move) & 7) * SIDE + me_z
        else:
            dest = me_y * SIDE + ((me_z + move) & 7)
        out.append(lookup(((dest * 2 + back_t) * 8 + hop) * 16 + i, ((owner * 2 + back2) * 8 + dist2) * 16 + pos2, loc, -1))
        out.append(lookup(me * 16 + t, owner * 16 + places[4], jnp.where(dist2 == 0, loc, 128 + jnp.minimum(back2 * 16 + pos2, 31)), 0))
    out.append(lookup(me * 16 + t, ln, acc, 0))
    out.append(out[-1])
    r = lax.broadcasted_iota(jnp.int32, (8, 128), 0)
    table = jnp.zeros((8, 128), jnp.int32)
    for k in range(7):
        table = jnp.where(r == k, out[k], table)
    return table


def table_kernel(dealing_ref, owners_ref, accepted_ref, table_ref, count_ref, columns):
    me = lax.axis_index("wide")
    ln, sender, owner, acc, me_y, me_z, halves, keys, starts, stacked = table_values(
        dealing_ref[...], owners_ref[...], accepted_ref[...], me
    )
    columns[...] = jnp.transpose(stacked)
    total = ln.shape[1]
    chunk = 64

    def count(step, found):
        part = columns[pl.ds(pl.multiple_of(step * chunk, chunk), chunk), :]
        return tuple(
            found[k]
            + jnp.sum(
                jnp.where(part[:, k : k + 1] < keys[k], 1.0, 0.0),
                axis=0,
                keepdims=True,
            )
            for k in range(5)
        )

    found = lax.fori_loop(
        0, total // chunk, count, tuple(jnp.zeros((1, total), F32) for _ in range(5))
    )
    table_ref[...] = finish_tables(
        ln, sender, owner, acc, me, halves, places_of(found, starts)
    )
    tokens = count_ref.shape[0]
    slot = lax.broadcasted_iota(jnp.int32, (tokens, total), 0) >> 4
    at = lax.broadcasted_iota(jnp.int32, (tokens, total), 1)
    count_ref[...] = jnp.sum(
        jnp.where(at == me * 16 + slot, acc, 0).astype(F32), axis=1, keepdims=True
    ).astype(jnp.int32)


CAPS = (16, 16, 12, 4)
OFFS = (0, 16, 32, 44)
SECOND_OFFS = (0, 4, 16, 32)


class Route:
    def __init__(self, number, table, refs, send_sem, recv_sem, side):
        self.number, self.table = number, table
        self.send_sem, self.recv_sem, self.side = send_sem, recv_sem, side
        self.pool, self.lists, self.passing, self.final, self.second = refs

    def neighbour(self, half, back, phase):
        me = lax.axis_index("wide")
        side = self.side
        y, z = me // side, lax.rem(me, side)
        move = side - 1 if back else 1
        if (half == 0) == (phase == 0):
            return y * side + lax.rem(z + move, side)
        return lax.rem(y + move, side) * side + z

    def copy(self, phase, half, back, hop):
        if phase == 0:
            low = 16 + 48 * back
            if hop == 0:
                source = self.lists.at[half, back]
            else:
                source = self.pool.at[half, pl.ds(low + OFFS[hop - 1], CAPS[hop])]
            target = self.pool.at[half, pl.ds(low + OFFS[hop], CAPS[hop])]
        else:
            size = CAPS[3 - hop]
            source = self.second.at[half, back, pl.ds(SECOND_OFFS[hop], size)]
            if hop < 3:
                target = self.passing.at[half, back, pl.ds(SECOND_OFFS[hop], size)]
            else:
                target = self.final.at[half, pl.ds(16 * back, size)]
        at = (((self.number * 2 + phase) * 2 + half) * 2 + back) * 4 + hop
        return pltpu.make_async_remote_copy(
            src_ref=source,
            dst_ref=target,
            send_sem=self.send_sem.at[at],
            recv_sem=self.recv_sem.at[at],
            device_id={"wide": self.neighbour(half, back, phase)},
            device_id_type=MESH,
        )

    def each(self, phase, hop):
        return [self.copy(phase, half, back, hop) for half in (0, 1) for back in (0, 1)]

    def fill(self, blocks, rows):
        for half in (0, 1):
            low = half * rows

            def own(i, carry):
                self.pool[half, i] = blocks[i, low : low + rows, :]
                return carry

            lax.fori_loop(0, 16, own, 0)
            for back in (0, 1):

                def listed(i, carry):
                    self.lists[half, back, i] = blocks[jnp.clip(self.table[3 * half, 16 * back + i], 0, 15), low : low + rows, :]
                    return carry

                lax.fori_loop(0, 16, listed, 0)

    def first(self, hop):
        if hop > 0:
            for copy in self.each(0, hop - 1):
                copy.wait_recv()
        if hop < 4:
            for copy in self.each(0, hop):
                copy.start()

    def after(self, hop):
        if hop > 0:
            for copy in self.each(1, hop - 1):
                copy.wait_recv()
        if hop == 4:
            return
        low = SECOND_OFFS[hop]
        size = CAPS[3 - hop]
        known = CAPS[4 - hop] if hop > 0 else 0
        for half in (0, 1):
            for back in (0, 1):

                def merged(i, carry):
                    at = self.table[3 * half + 1, 48 * back + low + i]
                    mine = self.pool[half, jnp.clip(at, 0, 111)]
                    came = self.passing[half, back, SECOND_OFFS[hop - 1] + i]
                    self.second[half, back, low + i] = jnp.where(at >= 0, mine, came)
                    return carry

                def fresh(i, carry):
                    at = self.table[3 * half + 1, 48 * back + low + i]
                    self.second[half, back, low + i] = self.pool[half, jnp.clip(at, 0, 111)]
                    return carry

                if known:
                    lax.fori_loop(0, known, merged, 0)
                if known < size:
                    lax.fori_loop(known, size, fresh, 0)
        for copy in self.each(1, hop):
            copy.start()

    def collect(self, blocks, rows):
        for half in (0, 1):
            low = half * rows

            def take(k, carry):
                at = self.table[3 * half + 2, k]
                here = self.pool[half, jnp.clip(jnp.where(at < 128, at, 0), 0, 111)]
                came = self.final[half, jnp.clip(at - 128, 0, 31)]
                blocks[k, low : low + rows, :] = jnp.where(at < 128, here, came)
                return carry

            lax.fori_loop(0, 16, take, 0)

    def drain(self):
        for phase in (0, 1):
            for hop in range(4):
                for copy in self.each(phase, hop):
                    copy.wait_send()


def layer_kernel(
    count,
    side,
    table_ref,
    bias_ref,
    decay_ref,
    skip_ref,
    acc_ref,
    hidden_ref,
    start_ref,
    tail_inner_ref,
    tail_shared_ref,
    gain_ref,
    w_gate_inner_ref,
    w_shared_ref,
    w_step_ref,
    conv_inner_ref,
    conv_inner_bias_ref,
    conv_shared_ref,
    conv_shared_bias_ref,
    gated_gain_ref,
    w_out_ref,
    next_gain_ref,
    w_next_ref,
    new_ref,
    next_ref,
    kept_ref,
    kept_inner_ref,
    kept_shared_ref,
    gather_buf,
    small_out,
    small_buf,
    square_out,
    square_buf,
    part_out,
    part_buf,
    new_buf,
    stack,
    message,
    state_out,
    state_pool,
    state_lists,
    state_passing,
    state_final,
    state_second,
    news_pool,
    news_lists,
    news_passing,
    news_final,
    news_second,
    send_sem,
    recv_sem,
    route_send,
    route_recv,
):
    me = lax.axis_index("narrow")
    states = Route(
        0,
        table_ref,
        (state_pool, state_lists, state_passing, state_final, state_second),
        route_send,
        route_recv,
        side,
    )
    updates = Route(
        1,
        table_ref,
        (news_pool, news_lists, news_passing, news_final, news_second),
        route_send,
        route_recv,
        side,
    )
    block, tokens = hidden_ref.shape
    requests = start_ref.shape[0]
    length = tokens // requests
    width = block * count
    barrier = pltpu.get_barrier_semaphore()
    for step in range(1, count):
        pl.semaphore_signal(
            barrier, inc=1, device_id={"narrow": lax.rem(me + step, count)}, device_id_type=MESH
        )
    for half in (0, 1):
        for back in (0, 1):
            pl.semaphore_signal(
                barrier,
                inc=1,
                device_id={"wide": states.neighbour(half, back, 0)},
                device_id_type=MESH,
            )
    pl.semaphore_wait(barrier, count + 3)

    def send(source, target_buf, stage, step):
        pltpu.make_async_remote_copy(
            src_ref=source,
            dst_ref=target_buf.at[me],
            send_sem=send_sem.at[stage],
            recv_sem=recv_sem.at[stage],
            device_id={"narrow": lax.rem(me + step, count)},
            device_id_type=MESH,
        ).start()

    def finish(target_buf, stage):
        some = target_buf.at[pl.ds(0, count - 1)]
        both = pltpu.make_async_remote_copy(
            src_ref=some,
            dst_ref=some,
            send_sem=send_sem.at[stage],
            recv_sem=recv_sem.at[stage],
            device_id={"narrow": lax.rem(me + 1, count)},
            device_id_type=MESH,
        )
        both.wait_recv()
        both.wait_send()

    for step in range(1, count):
        send(hidden_ref, gather_buf, 0, step)
    gather_buf[me] = hidden_ref[...]
    half_rows = start_ref.shape[1] // 2
    states.fill(start_ref, half_rows)
    states.first(0)

    rows = lax.broadcasted_iota(jnp.int32, (tokens, tokens), 0)
    cols = lax.broadcasted_iota(jnp.int32, (tokens, tokens), 1)
    same = (rows >> 4) == (cols >> 4)
    tri = same & (cols <= rows)
    eye = rows == cols
    place = rows[:, :1] & (length - 1)
    acc = acc_ref[...]
    lane = lax.broadcasted_iota(jnp.int32, (tokens, block), 1)
    small_eye = lax.broadcasted_iota(jnp.int32, (block, block), 0) == lax.broadcasted_iota(
        jnp.int32, (block, block), 1
    )
    turn = small_eye.astype(BF16)

    def to_row(column):
        return jnp.sum(jnp.where(eye, column, 0.0), axis=0, keepdims=True)

    def gain_column(gains, n):
        return jnp.sum(
            jnp.where(small_eye, gains[:, n * block : (n + 1) * block], 0.0), axis=1, keepdims=True
        )

    def spread(values):
        return jnp.where(
            lane < 64, values[:, 0:1], jnp.where(lane < 128, values[:, 1:2], values[:, 2:3])
        )

    def scalars(ref, where, limit):
        return jnp.where(where < limit, ref[0], jnp.where(where < 2 * limit, ref[1], ref[2]))

    def normed(buf, gains):
        total = jnp.zeros((1, tokens), F32)
        for n in range(count):
            piece = buf[n].astype(F32)
            total = total + jnp.sum(piece * piece, axis=0, keepdims=True)
        factor = lax.rsqrt(total / width + EPSILON)
        for n in range(count):
            stack[n * block : (n + 1) * block, :] = (
                buf[n].astype(F32) * factor * gains[n]
            ).astype(BF16)

    gains_now = gain_ref[...].reshape(1, width)
    gains_now = [gain_column(gains_now, n) for n in range(count)]
    states.first(1)
    finish(gather_buf, 0)
    normed(gather_buf, gains_now)
    upright = (((0,), (0,)), ((), ()))
    small_out[...] = bdot(w_shared_ref[...], stack[...]).astype(BF16)
    for step in range(1, count):
        send(small_out, small_buf, 1, step)
    small_buf[me] = small_out[...]
    step_raw = bdot(w_step_ref[...], stack[...]).astype(BF16)
    both = lax.dot_general(
        w_gate_inner_ref[...], stack[...], upright, preferred_element_type=F32
    ).astype(BF16)
    gate = lax.dot_general(both[:block], turn, upright, preferred_element_type=F32)
    inner_bf = lax.dot_general(both[block:], turn, upright, preferred_element_type=F32).astype(BF16)
    states.first(2)

    def filtered(fresh, tail, weight, offset):
        total = offset + fresh * weight[3:4]
        for shift in (1, 2, 3):
            moved = jnp.where(
                place >= shift,
                pltpu.roll(fresh, shift, 0),
                pltpu.roll(tail, tokens - length + shift, 0),
            )
            total = total + moved * weight[3 - shift : 4 - shift]
        return jax.nn.silu(total)

    def padded(ref):
        total = jnp.zeros((tokens, ref.shape[2]), F32)
        at = lax.broadcasted_iota(jnp.int32, (tokens, requests), 0)
        slot = lax.broadcasted_iota(jnp.int32, (tokens, requests), 1)
        kept_rows = ref.shape[0]
        for q in range(kept_rows):
            put = ((at >> 4) == slot) & ((at & (length - 1)) == length - kept_rows + q)
            total = total + bdot(put.astype(BF16), ref[q])
        return total.astype(BF16)

    tail_inner = padded(tail_inner_ref)
    tail_shared = padded(tail_shared_ref)
    conv_i = filtered(
        inner_bf.astype(F32),
        tail_inner.astype(F32),
        conv_inner_ref[...].astype(F32),
        conv_inner_bias_ref[...],
    )

    heads = w_step_ref.shape[0]
    head_lane = lax.broadcasted_iota(jnp.int32, (heads, 128), 1)
    head_eye = (head_lane == lax.broadcasted_iota(jnp.int32, (heads, 128), 0)).astype(BF16)
    lane_row = lax.broadcasted_iota(jnp.int32, (1, 128), 1)
    raw = lax.dot_general(step_raw, head_eye, upright, preferred_element_type=F32) + scalars(
        bias_ref, lane_row, 1
    )
    steps = jnp.maximum(raw, 0.0) + jnp.log1p(jnp.exp(-jnp.abs(raw)))
    log_decay = steps * -jnp.exp(scalars(decay_ref, lane_row, 1))
    cumul = fdot(tri.astype(F32), log_decay)
    col_place = cols & (length - 1)
    ending = fdot((same & (col_place < acc)).astype(F32), log_decay)
    before = place < acc
    factor = jnp.where(before, jnp.exp(jnp.where(before, ending - cumul, 0.0)), 0.0) * steps
    decayed = jnp.exp(ending)
    weighted = (conv_i * spread(factor)).astype(BF16)

    states.first(3)
    finish(small_buf, 1)
    shared = lax.dot_general(
        small_buf[...].reshape(tokens, tokens),
        eye.astype(BF16),
        upright,
        preferred_element_type=F32,
    )
    conv_s = filtered(
        shared, tail_shared.astype(F32), conv_shared_ref[...].astype(F32), conv_shared_bias_ref[...]
    )
    b_part = conv_s[:, :128]
    c_part = conv_s[:, 128:]
    states.first(4)
    states.after(0)

    edge = rows[:, :1] & 15
    wanted = jnp.where(
        edge < 3, edge, jnp.where(edge < 6, edge - 3, jnp.where(edge < 9, edge - 6, edge - 9))
    )
    target = acc + wanted - 3
    sel_fresh = (same & (col_place == target)).astype(BF16)
    sel_tail = (same & (col_place == target + length)).astype(BF16)
    edge_i = bdot(sel_fresh, inner_bf) + bdot(sel_tail, tail_inner)
    edge_s = bdot(sel_fresh, shared.astype(BF16)) + bdot(sel_tail, tail_shared)
    pick_in = lax.broadcasted_iota(jnp.int32, (block, 128), 0)
    pick_out = lax.broadcasted_iota(jnp.int32, (block, 128), 1)
    last_head = (pick_in == pick_out + 128).astype(BF16)
    high = decayed.astype(BF16).astype(F32)
    low = decayed - high
    edges = jnp.where(
        edge < 3,
        edge_i[:, :128],
        jnp.where(
            edge < 6,
            bdot(edge_i.astype(BF16), last_head),
            jnp.where(
                edge < 9,
                edge_s[:, :128],
                jnp.where(
                    edge < 12, edge_s[:, 128:], jnp.where(edge == 12, high, jnp.where(edge == 13, low, 0.0))
                ),
            ),
        ),
    )
    message[:, 0:16, :] = weighted[:, :128].reshape(requests, length, 128)
    message[:, 16:32, :] = bdot(weighted, last_head).astype(BF16).reshape(requests, length, 128)
    message[:, 32:48, :] = b_part.astype(BF16).reshape(requests, length, 128)
    message[:, 48:64, :] = edges.astype(BF16).reshape(requests, length, 128)

    updates.fill(message, 32)
    updates.first(0)
    states.after(1)

    crossing = lax.dot_general(
        c_part.astype(BF16), b_part.astype(BF16), (((1,), (1,)), ((), ())), preferred_element_type=F32
    )
    direct = jnp.zeros((tokens, block), F32)
    for head in range(3):
        column = cumul[:, head : head + 1]
        gap = jnp.where(tri, column - to_row(column), 0.0)
        mixing = jnp.where(tri, jnp.exp(gap), 0.0) * to_row(steps[:, head : head + 1]) * crossing
        direct = direct + bdot(
            mixing.astype(BF16), jnp.where((lane >> 6) == head, conv_i, 0.0).astype(BF16)
        )
    updates.first(1)
    carried = lax.dot_general(
        c_part.astype(BF16).reshape(requests, length, 128),
        start_ref[...],
        (((2,), (2,)), ((0,), (0,))),
        preferred_element_type=F32,
    ).reshape(tokens, block)
    outputs = carried * spread(jnp.exp(cumul)) + direct + scalars(skip_ref, lane, 64) * conv_i
    gated = outputs * jax.nn.silu(gate)
    square_out[...] = lax.dot_general(
        jnp.ones((8, block), F32),
        gated * gated,
        (((1,), (1,)), ((), ())),
        precision=HIGHEST,
        preferred_element_type=F32,
    )
    for step in range(1, count):
        send(square_out, square_buf, 2, step)
    square_buf[me] = square_out[...]
    scaled = (gated * gated_gain_ref[...]).astype(BF16)
    scaled = lax.dot_general(
        turn, scaled, (((1,), (1,)), ((), ())), preferred_element_type=F32
    ).astype(BF16)
    part_out[...] = (
        lax.dot_general(w_out_ref[...], scaled, upright, preferred_element_type=F32)
        .astype(BF16)
        .reshape(count, block, tokens)
    )
    for step in range(1, count):
        send(part_out.at[lax.rem(me + step, count)], part_buf, 3, step)
    part_buf[me] = part_out[me]

    updates.first(2)
    states.after(2)
    updates.first(3)
    updates.first(4)
    updates.after(0)
    finish(square_buf, 2)
    squares = square_buf[0]
    for n in range(1, count):
        squares = squares + square_buf[n]
    factor_out = lax.rsqrt(squares[0:1] / width + EPSILON)
    finish(part_buf, 3)
    summed = part_buf[0].astype(F32)
    for n in range(1, count):
        summed = summed + part_buf[n].astype(F32)
    new_ref[...] = (hidden_ref[...].astype(F32) + summed * factor_out).astype(BF16)
    for step in range(1, count):
        send(new_ref, new_buf, 4, step)
    new_buf[me] = new_ref[...]
    updates.after(1)
    states.after(3)
    updates.after(2)
    updates.after(3)
    states.after(4)
    updates.after(4)
    states.collect(state_out, half_rows)
    updates.collect(message, 32)
    over = (((1,), (1,)), ((0,), (0,)))
    b_rows = message[:, 32:48, :]
    first = lax.dot_general(message[:, 0:16, :], b_rows, over, preferred_element_type=F32)
    last = lax.dot_general(message[:, 16:32, :], b_rows, over, preferred_element_type=F32)
    edges = message[:, 48:64, :].astype(F32)
    swap = ((rows >> 4) == (cols & 15)) & ((rows & 15) == (cols >> 4))
    by_row = bdot(swap.astype(BF16), message[:, 48:64, :].reshape(tokens, 128)).astype(BF16)
    for q in range(3):
        kept_inner_ref[q, :, 0:128] = by_row[16 * q : 16 * q + 16]
        kept_inner_ref[q, :, 128:192] = by_row[48 + 16 * q : 64 + 16 * q, 0:64]
        kept_shared_ref[q, :, 0:128] = by_row[96 + 16 * q : 112 + 16 * q]
        kept_shared_ref[q, :, 128:256] = by_row[144 + 16 * q : 160 + 16 * q]
    decay = edges[:, 12:13, :] + edges[:, 13:14, :]
    for head in range(3):
        low = 64 * head
        added = first[:, low : low + 64, :] if head < 2 else last[:, 0:64, :]
        kept_ref[:, low : low + 64, :] = (
            state_out[:, low : low + 64, :].astype(F32) * decay[:, :, head : head + 1] + added
        ).astype(BF16)
    finish(new_buf, 4)
    gains_next = next_gain_ref[...].reshape(1, width)
    normed(new_buf, [gain_column(gains_next, n) for n in range(count)])
    next_ref[...] = bdot(w_next_ref[...], stack[...]).astype(BF16)
    states.drain()
    updates.drain()


def hand_over_kernel(*refs):
    half = len(refs) // 2
    for source, target in zip(refs[:half], refs[half:]):
        target[...] = source[...]


def whole(memory_space=pltpu.VMEM):
    return pl.BlockSpec(memory_space=memory_space)


def local(
    count,
    hidden,
    start_state,
    tail_inner,
    tail_shared,
    input_gain,
    w_gate_inner,
    w_shared,
    w_step,
    step_bias,
    decay_log,
    conv_inner,
    conv_inner_bias,
    conv_shared,
    conv_shared_bias,
    skip_gain,
    gated_gain,
    w_output,
    next_gain,
    w_next,
    dealing,
    accepted,
    owners,
):
    tokens, block = hidden.shape
    requests, heads, head_size, states = start_state.shape
    start = start_state.reshape(requests, heads * head_size, states)
    routed = []
    for rows in (heads * head_size // 2, 32):
        routed += [
            pltpu.VMEM((2, 112, rows, 128), BF16),
            pltpu.VMEM((2, 2, 16, rows, 128), BF16),
            pltpu.VMEM((2, 2, 32, rows, 128), BF16),
            pltpu.VMEM((2, 32, rows, 128), BF16),
            pltpu.VMEM((2, 2, 48, rows, 128), BF16),
        ]
    shared_here = w_shared.shape[1]
    table, accepted_rows = pl.pallas_call(
        table_kernel,
        out_shape=(
            jax.ShapeDtypeStruct((8, 128), jnp.int32),
            jax.ShapeDtypeStruct((tokens, 1), jnp.int32),
        ),
        in_specs=[whole()] * 3,
        out_specs=(whole(), whole()),
        scratch_shapes=[pltpu.VMEM((dealing.shape[0], 8), F32)],
    )(dealing[None, :], owners[None, :], accepted[None, :])
    operands = (
        table,
        step_bias,
        decay_log,
        skip_gain,
        accepted_rows,
        hidden.T,
        start,
        tail_inner.transpose(1, 0, 2),
        tail_shared.transpose(1, 0, 2),
        input_gain,
        w_gate_inner,
        w_shared.T,
        w_step.T,
        conv_inner,
        conv_inner_bias[None, :],
        conv_shared,
        conv_shared_bias[None, :],
        gated_gain[None, :],
        w_output,
        next_gain,
        w_next.T,
    )
    blocks = pltpu.VMEM((count, block, tokens), BF16)
    results = pl.pallas_call(
        functools.partial(layer_kernel, count, SIDE),
        out_shape=(
            jax.ShapeDtypeStruct((block, tokens), BF16),
            jax.ShapeDtypeStruct((w_next.shape[1], tokens), BF16),
            jax.ShapeDtypeStruct(start.shape, BF16),
            jax.ShapeDtypeStruct((3, requests, tail_inner.shape[2]), BF16),
            jax.ShapeDtypeStruct((3, requests, tail_shared.shape[2]), BF16),
        ),
        in_specs=[whole(pltpu.SMEM)] * 4 + [whole()] * (len(operands) - 4),
        out_specs=(whole(),) * 5,
        scratch_shapes=[
            blocks,
            pltpu.VMEM((shared_here, tokens), BF16),
            pltpu.VMEM((count, shared_here, tokens), BF16),
            pltpu.VMEM((8, tokens), F32),
            pltpu.VMEM((count, 8, tokens), F32),
            blocks,
            blocks,
            blocks,
            pltpu.VMEM((count * block, tokens), BF16),
            pltpu.VMEM((requests, 64, 128), BF16),
            pltpu.VMEM(start.shape, BF16),
            *routed,
            pltpu.SemaphoreType.DMA((5,)),
            pltpu.SemaphoreType.DMA((5,)),
            pltpu.SemaphoreType.DMA((64,)),
            pltpu.SemaphoreType.DMA((64,)),
        ],
        compiler_params=pltpu.CompilerParams(
            collective_id=0, has_side_effects=True, vmem_limit_bytes=58 << 20
        ),
        cost_estimate=pl.CostEstimate(
            flops=4_000_000_000, bytes_accessed=100_000_000, transcendentals=0
        ),
    )(*operands)
    new_part, next_input, kept, kept_inner, kept_shared = pl.pallas_call(
        hand_over_kernel,
        out_shape=tuple(jax.ShapeDtypeStruct(one.shape, one.dtype) for one in results),
        in_specs=[whole()] * 5,
        out_specs=(whole(),) * 5,
    )(*results)
    return (
        new_part.T,
        next_input.T,
        kept.reshape(start_state.shape),
        kept_inner.transpose(1, 0, 2),
        kept_shared.transpose(1, 0, 2),
    )


def solution(mesh):
    placed = (
        P("wide", "narrow"),
        P("wide", "narrow", None, None),
        P("wide", None, "narrow"),
        P("wide", None, None),
        P(),
        P(None, "narrow"),
        P(None, "narrow"),
        P(None, "narrow"),
        P("narrow"),
        P("narrow"),
        P(None, "narrow"),
        P("narrow"),
        P(),
        P(),
        P("narrow"),
        P("narrow"),
        P("narrow", None),
        P(),
        P(None, "narrow"),
        P(),
        P(),
        P(),
    )
    return jax.shard_map(
        functools.partial(local, mesh.shape["narrow"]),
        mesh=mesh,
        in_specs=placed,
        out_specs=(
            P("wide", "narrow"),
            P("wide", "narrow"),
            P("wide", "narrow", None, None),
            P("wide", None, "narrow"),
            P("wide", None, None),
        ),
        check_vma=False,
    )
```
